128 devices in a mesh: ctx: 32 (over x, z_hi, y), ch: 2 (over z_lo), section: 2 (over core).
Axes of the slice: x: 4, y: 4, z: 4 (z_hi: 2, z_lo: 2; z = z_hi * 2 + z_lo), core: 2. Of those that a mesh axis runs over, the one named last changes fastest.
Arguments:
- mamba_x: bfloat16 [4096, 8192], P('ctx', ('ch', 'section')), may hold values from -6 to 6
- mamba_b: bfloat16 [4096, 1024], P('ctx', ('ch', 'section')), may hold values from -6 to 6
- mamba_c: bfloat16 [4096, 1024], P('ctx', ('ch', 'section')), may hold values from -6 to 6
- step_dt: float32 [4096, 64], P('ctx', ('ch', 'section')), may hold values from 0 to 0.35, as said below
- decay_a: float32 [64], P(('ch', 'section')), may hold values from 0.5 to 2
- skip_d: float32 [64], P(('ch', 'section')), may hold values from 0.5 to 1.5
- value_weight: bfloat16 [8192, 1024], P(('ch', 'section')), may hold values from -0.0625 to 0.0625
- queries: bfloat16 [4096, 8192], P('ctx', ('ch', 'section')), may hold values from -20 to 20
- keys: bfloat16 [4096, 1024], P('ctx', ('ch', 'section')), may hold values from -6 to 6
- out_grad: bfloat16 [4096, 8192], P('ctx', ('ch', 'section')), may hold values from -6 to 6
Outputs:
- attn_out: float32 [4096, 8192], P('ctx', ('ch', 'section'))
- grad_q: float32 [4096, 8192], P('ctx', ('ch', 'section'))
- grad_k: float32 [4096, 1024], P('ctx', ('ch', 'section'))
- grad_x: float32 [4096, 8192], P('ctx', ('ch', 'section'))
- grad_b: float32 [4096, 1024], P('ctx', ('ch', 'section'))
- grad_c: float32 [4096, 1024], P('ctx', ('ch', 'section'))
The draws below stay inside these ranges and needn't reach their ends.
Inputs may be any that keep to these rules, and one draw needn't show every extreme that they name: `step_dt`: positive step sizes.
All inputs are finite; a program needn't handle non-finite values.
Results may differ from the reference program's by a relative error of at most 0.0059.
Values may be sent and summed in bfloat16 or wider, within the bound.
No kernel may reach another device: no remote copies, remote signals or barrier semaphores. Data moves between devices by JAX's collectives and lax.ppermute only.
A program may use at most 128 MiB of HBM per device.

```python
import math
import jax
import jax.numpy as jnp
from jax import lax

TOK_DEV = 128
SSM_HEADS = 64
HEAD_P = 128
STATE = 128
GROUPS = 8
Q_HEADS = 64
KV_HEADS = 8
HEAD_DIM = 128
CONTEXT_LENGTH = 4096


def key_field(key):
    base_key = jax.random.fold_in(key, 21)
    field = jax.random.truncated_normal(base_key, -6.0, 6.0, (CONTEXT_LENGTH, KV_HEADS, HEAD_DIM), jnp.float32)
    return field


def draw_keys(key, part):
    field = key_field(key)
    return field.reshape(CONTEXT_LENGTH, KV_HEADS * HEAD_DIM).astype(jnp.bfloat16)


def draw_queries(key, part):
    base_key = jax.random.fold_in(key, 22)
    field = jax.random.truncated_normal(base_key, -6.0, 6.0, (CONTEXT_LENGTH, Q_HEADS, HEAD_DIM), jnp.float32)
    return field.reshape(CONTEXT_LENGTH, Q_HEADS * HEAD_DIM).astype(jnp.bfloat16)


def draw_step_dt(key, part):
    sub_keys = jax.random.split(key, 3)
    fast_share = 0.5
    fast_heads = jax.random.uniform(sub_keys[0], (SSM_HEADS,), jnp.float32) < fast_share
    stochastic_jitter = jnp.exp(jax.random.uniform(sub_keys[1], (CONTEXT_LENGTH, SSM_HEADS), jnp.float32, -math.log(2.0), math.log(2.0)))
    nominal_frequency = jnp.where(fast_heads, 1.0 / 40.0, 0.5 / CONTEXT_LENGTH)
    flagged_locations = jax.random.randint(sub_keys[2], (4,), 0, CONTEXT_LENGTH)
    clustered_arrivals = jnp.any(jnp.arange(CONTEXT_LENGTH)[:, None] == flagged_locations[None, :], axis=1)
    return nominal_frequency[None, :] * stochastic_jitter + jnp.where(clustered_arrivals, 0.3, 0.0)[:, None]


def block_scale(own_key, extent, cuts, least, largest):
    def one(dim, blocks):
        heights = jax.random.uniform(jax.random.fold_in(jax.random.fold_in(own_key, 6), dim), (blocks,), jnp.float32, least / len(cuts), largest / len(cuts))
        return jnp.repeat(jnp.exp(heights), extent[dim] // blocks).reshape((-1,) + (1,) * (len(extent) - dim - 1))

    factor_of = one(*cuts[0])
    for cut in cuts[1:]:
        factor_of = factor_of * one(*cut)
    return factor_of


def scatter_about(rng, extent, width, limit, cuts=(), kind=jnp.bfloat16):
    result = jax.random.normal(rng, extent, jnp.float32) * width
    if len(cuts) > 0:
        result = block_scale(rng, extent, cuts, -0.22, 0.18) * result
    return jnp.clip(result, min=-limit, max=limit).astype(kind)


def setup_inputs(seed: int = 0) -> dict:
    arg_keys = jax.random.split(jax.random.key(seed), 11)
    mamba_x = scatter_about(arg_keys[0], (CONTEXT_LENGTH, SSM_HEADS * HEAD_P), 1.0, 6.0, ((0, 32), (1, 4)))
    mamba_b = scatter_about(arg_keys[1], (CONTEXT_LENGTH, GROUPS * STATE), 1.0, 6.0, ((0, 32), (1, 4)))
    mamba_c = scatter_about(arg_keys[2], (CONTEXT_LENGTH, GROUPS * STATE), 1.0, 6.0, ((0, 32), (1, 4)))
    step_dt = draw_step_dt(jax.random.fold_in(arg_keys[10], 71), 0)
    decay_a = jnp.clip(jnp.exp(math.log(2.0) - 1.3862944 * jax.random.uniform(arg_keys[4], (SSM_HEADS,), jnp.float32) ** block_scale(arg_keys[4], (SSM_HEADS,), ((0, 4),), -0.2, 0.2)), 0.5, 2.0)
    skip_d = jnp.clip(0.5 + 1.0 * jax.random.uniform(arg_keys[5], (SSM_HEADS,), jnp.float32) ** block_scale(arg_keys[5], (SSM_HEADS,), ((0, 4),), -0.2, 0.2), 0.5, 1.5)
    value_weight = scatter_about(arg_keys[6], (SSM_HEADS * HEAD_P, KV_HEADS * HEAD_DIM), (SSM_HEADS * HEAD_P) ** -0.5, 0.0625, ((0, 4),))
    queries = draw_queries(jax.random.fold_in(arg_keys[10], 71), 0)
    keys = draw_keys(jax.random.fold_in(arg_keys[10], 71), 0)
    out_grad = scatter_about(arg_keys[9], (CONTEXT_LENGTH, Q_HEADS * HEAD_DIM), 1.0, 6.0, ((0, 32), (1, 4)))
    return dict(mamba_x=mamba_x, mamba_b=mamba_b, mamba_c=mamba_c, step_dt=step_dt, decay_a=decay_a, skip_d=skip_d, value_weight=value_weight, queries=queries, keys=keys, out_grad=out_grad)


HIGHEST = lax.Precision.HIGHEST
NEG_FILL = -1e+30

def block_terms(inputs_x, inputs_b, inputs_c, step_sizes, decay_rates, skip_gains):
    head_count = inputs_x.shape[1]
    repeat_by = head_count // inputs_b.shape[1]
    log_sums = jnp.cumsum(-step_sizes * decay_rates[None, :], axis=0)
    positions = jnp.arange(log_sums.shape[0])
    lower_mask = (positions[:, None] >= positions[None, :])[None]
    log_gaps = log_sums.T[:, :, None] - log_sums.T[:, None, :]
    decays = jnp.where(lower_mask, jnp.exp(jnp.where(lower_mask, log_gaps, 0.0)), 0.0)
    inner_prod = jnp.einsum('tgn,sgn->gts', inputs_c, inputs_b, precision=HIGHEST)
    inner_prod = jnp.repeat(inner_prod, repeat_by, axis=0)
    mixing = inner_prod * decays * step_sizes.T[:, None, :]
    local_out = jnp.einsum('hts,shp->thp', mixing, inputs_x, precision=HIGHEST) + skip_gains[None, :, None] * inputs_x
    to_end = jnp.exp(log_sums[-1][None, :] - log_sums) * step_sizes
    b_heads = jnp.repeat(inputs_b, repeat_by, axis=1)
    weighted = inputs_x * to_end[:, :, None]
    end_state = jnp.einsum('shp,shn->hpn', weighted, b_heads, precision=HIGHEST)
    return (local_out, end_state, jnp.exp(log_sums[-1]))

def entry_terms(inputs_c, step_sizes, decay_rates, entering):
    repeat_by = entering.shape[0] // inputs_c.shape[1]
    log_sums = jnp.cumsum(-step_sizes * decay_rates[None, :], axis=0)
    c_heads = jnp.repeat(inputs_c, repeat_by, axis=1)
    carried = jnp.einsum('thn,hpn->thp', c_heads, entering, precision=HIGHEST)
    return jnp.exp(log_sums)[:, :, None] * carried

def mamba_forward(x_float, b_float, readout_matrix_single, step_dt, decay_a, skip_d):
    block_count = x_float.shape[0] // TOK_DEV
    x_blocks = x_float.reshape(block_count, TOK_DEV, SSM_HEADS, HEAD_P)
    b_blocks = b_float.reshape(block_count, TOK_DEV, GROUPS, STATE)
    c_blocks = readout_matrix_single.reshape(block_count, TOK_DEV, GROUPS, STATE)
    dt_blocks = step_dt.reshape(block_count, TOK_DEV, SSM_HEADS)
    local_out, end_states, end_decays = jax.vmap(block_terms, in_axes=(0, 0, 0, 0, None, None))(x_blocks, b_blocks, c_blocks, dt_blocks, decay_a, skip_d)

    def advance(running, item_pair):
        return (item_pair[0][:, None, None] * running + item_pair[1], running)
    initial = jnp.zeros((SSM_HEADS, HEAD_P, STATE), jnp.float32)
    _, entering = lax.scan(advance, initial, (end_decays, end_states))
    entry_out = jax.vmap(entry_terms, in_axes=(0, 0, None, 0))(c_blocks, dt_blocks, decay_a, entering)
    return (local_out + entry_out).reshape(x_float.shape[0], SSM_HEADS * HEAD_P)

def attend_group(group_q, group_k, group_v, group_d):
    scale_by = 1.0 / math.sqrt(HEAD_DIM)
    positions = jnp.arange(group_q.shape[0])
    visible = (positions[None, :] <= positions[:, None])[None]
    scores = jnp.einsum('trd,sd->rts', group_q, group_k) * scale_by
    scores = jnp.where(visible, scores, NEG_FILL)
    row_top = lax.optimization_barrier(jnp.max(scores, axis=-1))
    probs = jnp.where(visible, jnp.exp(scores - row_top[..., None]), 0.0)
    probs = probs / lax.optimization_barrier(jnp.sum(probs, axis=-1))[..., None]
    probability_batch = probs.astype(jnp.bfloat16).astype(jnp.float32)
    output = jnp.einsum('rts,sd->trd', probability_batch, group_v)
    dprobs = jnp.einsum('trd,sd->rts', group_d, group_v)
    delta = lax.optimization_barrier(jnp.sum(group_d * output, axis=-1)).T
    dscores = probs * (dprobs - delta[..., None])
    score_gradient_batch = dscores.astype(jnp.bfloat16).astype(jnp.float32)
    query_grad = jnp.einsum('rts,sd->trd', score_gradient_batch, group_k) * scale_by
    key_grad = jnp.einsum('rts,trd->sd', score_gradient_batch, group_q) * scale_by
    value_grad = jnp.einsum('rts,trd->sd', probability_batch, group_d).astype(jnp.bfloat16)
    return (output, query_grad, key_grad, value_grad)

def reference(mamba_x, mamba_b, mamba_c, step_dt, decay_a, skip_d, value_weight, queries, keys, out_grad):
    x_float = mamba_x.astype(jnp.float32)
    b_float = mamba_b.astype(jnp.float32)
    readout_matrix_single = mamba_c.astype(jnp.float32)

    def forward(arg_x, arg_b, arg_c):
        return mamba_forward(arg_x, arg_b, arg_c, step_dt, decay_a, skip_d)
    mamba_y, pullback = jax.vjp(forward, x_float, b_float, readout_matrix_single)
    values = jnp.dot(mamba_y.astype(jnp.bfloat16), value_weight, preferred_element_type=jnp.float32).astype(jnp.bfloat16)
    rep_count = Q_HEADS // KV_HEADS
    grouped_q = queries.astype(jnp.float32).reshape(CONTEXT_LENGTH, KV_HEADS, rep_count, HEAD_DIM).transpose(1, 0, 2, 3)
    grouped_d = out_grad.astype(jnp.float32).reshape(CONTEXT_LENGTH, KV_HEADS, rep_count, HEAD_DIM).transpose(1, 0, 2, 3)
    grouped_k = keys.astype(jnp.float32).reshape(CONTEXT_LENGTH, KV_HEADS, HEAD_DIM).transpose(1, 0, 2)
    grouped_v = values.astype(jnp.float32).reshape(CONTEXT_LENGTH, KV_HEADS, HEAD_DIM).transpose(1, 0, 2)
    outputs, query_grads, key_grads, value_grads = lax.map(lambda packed: attend_group(packed[0], packed[1], packed[2], packed[3]), (grouped_q, grouped_k, grouped_v, grouped_d))
    attn_out = outputs.transpose(1, 0, 2, 3).reshape(CONTEXT_LENGTH, Q_HEADS * HEAD_DIM)
    grad_q = query_grads.transpose(1, 0, 2, 3).reshape(CONTEXT_LENGTH, Q_HEADS * HEAD_DIM)
    grad_k = key_grads.transpose(1, 0, 2).reshape(CONTEXT_LENGTH, KV_HEADS * HEAD_DIM)
    value_grad = value_grads.transpose(1, 0, 2).reshape(CONTEXT_LENGTH, KV_HEADS * HEAD_DIM)
    mamba_grad = jnp.dot(value_grad, value_weight.T, preferred_element_type=jnp.float32)
    grad_x, grad_b, grad_c = pullback(mamba_grad)
    return (attn_out, grad_q, grad_k, grad_x, grad_b, grad_c)
```

```python
import math

import jax
import jax.numpy as jnp
from jax import lax
from jax.experimental import pallas as pl
from jax.experimental.pallas import tpu as pltpu
from jax.sharding import PartitionSpec as P

T = 128
NH = 16
GH = 8
F32 = jnp.float32
BF = jnp.bfloat16
HI = lax.Precision.HIGHEST
SCALE = 1.0 / math.sqrt(128.0)
SR = 64
DR = 16
NEG = -1e30

NN = (((1,), (0,)), ((), ()))
NT = (((1,), (1,)), ((), ()))
TN = (((0,), (0,)), ((), ()))


def mm(a, b, dims=NN):
    return lax.dot_general(a, b, dims, preferred_element_type=F32)


def mm_exact(a, b, dims=NN):
    return lax.dot_general(a, b, dims, precision=HI, preferred_element_type=F32)


def head(h):
    return slice(h * T, (h + 1) * T)


def lower_tri():
    row = lax.broadcasted_iota(jnp.int32, (T, T), 0)
    col = lax.broadcasted_iota(jnp.int32, (T, T), 1)
    return row >= col


def sums_by_token(dt_ref, a_ref):
    steps = -dt_ref[...] * a_ref[...]
    return mm_exact(lower_tri().astype(F32), steps)


def sums_by_head(dt_ref, a_ref):
    row = lax.broadcasted_iota(jnp.int32, (T, T), 0)
    col = lax.broadcasted_iota(jnp.int32, (T, T), 1)
    steps = -dt_ref[...] * a_ref[...]
    upper = (row <= col).astype(F32)
    same = (row == col).astype(F32)
    return mm_exact(steps, upper, TN), mm_exact(dt_ref[...], same, TN)


def state_kernel(x_ref, b_ref, dt_ref, a_ref, k_ref, out_ref):
    cum = sums_by_token(dt_ref, a_ref)
    total = cum[T - 1 : T, :]
    weight = jnp.exp(total - cum) * dt_ref[...]
    first = total.astype(BF).astype(F32)
    second = (total - first).astype(BF).astype(F32)
    third = total - first - second
    row = lax.broadcasted_iota(jnp.int32, (DR, T), 0)
    for h in range(NH):
        g = h // GH
        xw = (x_ref[:, head(h)].astype(F32) * weight[:, h : h + 1]).astype(BF)
        state = mm(xw, b_ref[:, head(g)], TN).astype(BF)
        parts = jnp.where(
            row == 0,
            first[:, h : h + 1],
            jnp.where(row == 1, second[:, h : h + 1], third[:, h : h + 1]),
        ).astype(BF)
        for half in range(2):
            d = 2 * h + half
            out_ref[d, 0:SR, :] = state[half * SR : (half + 1) * SR]
            out_ref[d, SR : SR + DR, :] = parts
    for d in range(32):
        out_ref[d, SR + DR : SR + DR + T, :] = k_ref[:, head(d // 16)]


def decay_of(r1_ref, c):
    parts = r1_ref[c, SR : SR + DR, :].astype(F32)
    return jnp.exp(parts[0:1] + parts[1:2] + parts[2:3])


def probs_kernel(
    at_ref, r1_ref, q_ref, d_ref, other_ref, pay_ref, p_ref, qs_ref, ds_ref, s_sc, dv_sc
):
    at = at_ref[0]
    upper = (at >= 16).astype(jnp.int32)
    low = jnp.minimum(at, 31 - at)

    run = jnp.zeros((SR, T), F32)
    for c in range(32):
        pay_ref[c, 0:SR, :] = run.astype(BF)
        run = decay_of(r1_ref, c) * run + r1_ref[c, 0:SR, :].astype(F32)

    for h in range(GH):
        own = pl.ds(pl.multiple_of(upper * 1024 + h * T, T), T)
        qs_ref[upper, head(h), :] = q_ref[:, own]
        ds_ref[upper, head(h), :] = d_ref[:, own]
        qs_ref[1 - upper, head(h), :] = other_ref[0:T, head(h)]
        ds_ref[1 - upper, head(h), :] = other_ref[T : 2 * T, head(h)]

    dv_sc[...] = jnp.zeros_like(dv_sc)
    key = lax.broadcasted_iota(jnp.int32, (T, 256), 0)
    tok = lax.broadcasted_iota(jnp.int32, (T, 256), 1) & (T - 1)
    seen = key <= tok

    for sel in range(2):
        count = low if sel == 0 else 31 - low
        base = 0 if sel == 0 else low + 1

        def scores(j, top, diag, sel=sel, base=base):
            k = r1_ref[j, SR + DR : SR + DR + T, :]
            tops = []
            for c in range(4):
                cols = slice(c * 256, (c + 1) * 256)
                s = mm(k, qs_ref[sel, cols, :], NT)
                if diag:
                    s = jnp.where(seen, s, NEG)
                s_sc[base + j, :, cols] = s
                tops.append(jnp.maximum(top[c], jnp.max(s.reshape(16, 8, 256), axis=0)))
            return tuple(tops)

        top = tuple(jnp.full((8, 256), NEG, F32) for _ in range(4))
        top = lax.fori_loop(0, count, lambda j, t: scores(j, t, False), top)
        top = scores(count, top, True)
        peak = [jnp.max(t, axis=0, keepdims=True) for t in top]

        def weigh(j, tot, base=base, peak=peak):
            tots = []
            for c in range(4):
                cols = slice(c * 256, (c + 1) * 256)
                p = jnp.exp((s_sc[base + j, :, cols] - peak[c]) * SCALE)
                s_sc[base + j, :, cols] = p
                tots.append(tot[c] + jnp.sum(p.reshape(16, 8, 256), axis=0))
            return tuple(tots)

        tot = tuple(jnp.zeros((8, 256), F32) for _ in range(4))
        tot = lax.fori_loop(0, count + 1, weigh, tot)
        inv = [1.0 / jnp.sum(t, axis=0, keepdims=True) for t in tot]

        def spread(j, none, sel=sel, base=base, inv=inv):
            acc = dv_sc[j]
            for c in range(4):
                cols = slice(c * 256, (c + 1) * 256)
                p = (s_sc[base + j, :, cols] * inv[c]).astype(BF)
                p_ref[base + j, :, cols] = p
                acc = acc + mm(p, ds_ref[sel, cols, :])
            dv_sc[j] = acc
            return none

        lax.fori_loop(0, count + 1, spread, 0)

    for c in range(32):
        pay_ref[c, SR : SR + T, :] = dv_sc[c].astype(BF)


def values_kernel(
    x_ref, b_ref, c_ref, dt_ref, a_ref, skip_ref, r2_ref, w_ref, out_ref, y_sc
):
    cum = sums_by_token(dt_ref, a_ref)
    cum_t, dt_t = sums_by_head(dt_ref, a_ref)
    grow = jnp.exp(cum)
    lower = lower_tri()
    for g in range(2):
        cb = mm(c_ref[:, head(g)], b_ref[:, head(g)], NT)
        for h in range(g * GH, (g + 1) * GH):
            gap = cum[:, h : h + 1] - cum_t[h : h + 1, :]
            mix = cb * jnp.exp(jnp.where(lower, gap, NEG)) * dt_t[h : h + 1, :]
            x = x_ref[:, head(h)]
            enter = jnp.concatenate([r2_ref[2 * h, 0:SR, :], r2_ref[2 * h + 1, 0:SR, :]], 0)
            y = mm(mix.astype(BF), x) + skip_ref[:, h : h + 1] * x.astype(F32)
            y = y + grow[:, h : h + 1] * mm(c_ref[:, head(g)], enter, NT)
            y_sc[:, head(h)] = y.astype(BF)
    dv = []
    for k in range(2):
        acc = r2_ref[16 * k, SR : SR + T, :].astype(F32)
        for s in range(1, 16):
            acc = acc + r2_ref[16 * k + s, SR : SR + T, :].astype(F32)
        dv.append(acc.astype(BF))
    for d in range(4):
        cols = slice(d * 256, (d + 1) * 256)
        out_ref[d, :, 0:256] = mm(y_sc[...], w_ref[:, cols]).astype(BF)
        out_ref[d, :, 256:384] = dv[0]
        out_ref[d, :, 384:512] = dv[1]


def back_kernel(r3_ref, w_ref, c_ref, dt_ref, a_ref, pay_ref, dy_ref):
    values = r3_ref[0, :, 0:256].astype(F32)
    for s in range(1, 4):
        values = values + r3_ref[s, :, 0:256].astype(F32)
    values = values.astype(BF)
    for d in range(32):
        pay_ref[d, SR : SR + T, :] = values[:, head(d // 16)]
    vg = jnp.concatenate([r3_ref[s, :, 256:512] for s in range(4)], axis=1)
    grow = jnp.exp(sums_by_token(dt_ref, a_ref))
    for h in range(NH):
        dy = mm(vg, w_ref[head(h), :], NT)
        dy_ref[:, head(h)] = dy
        eg = mm((dy * grow[:, h : h + 1]).astype(BF), c_ref[:, head(h // GH)], TN).astype(BF)
        pay_ref[2 * h, 0:SR, :] = eg[0:SR]
        pay_ref[2 * h + 1, 0:SR, :] = eg[SR:T]


def grads_kernel(
    at_ref, r1_ref, r4_ref, p_ref, qs_ref, ds_ref, pay_ref, o_ref, send_ref,
    dp_sc, o_sc, dq_sc, dk_sc
):
    at = at_ref[0]
    upper = (at >= 16).astype(jnp.int32)
    low = jnp.minimum(at, 31 - at)

    run = jnp.zeros((SR, T), F32)
    for c in range(31, -1, -1):
        pay_ref[c, 0:SR, :] = run.astype(BF)
        run = decay_of(r1_ref, c) * run + r4_ref[c, 0:SR, :].astype(F32)

    dk_sc[...] = jnp.zeros_like(dk_sc)
    o_sc[...] = jnp.zeros_like(o_sc)
    dq_sc[...] = jnp.zeros_like(dq_sc)
    for sel in range(2):
        count = low if sel == 0 else 31 - low
        base = 0 if sel == 0 else low + 1

        def first(j, delta, sel=sel, base=base):
            v = r4_ref[j, SR : SR + T, :]
            deltas = []
            for c in range(4):
                cols = slice(c * 256, (c + 1) * 256)
                p = p_ref[base + j, :, cols]
                dp = mm(v, ds_ref[sel, cols, :], NT)
                dp_sc[base + j, :, cols] = dp
                term = p.astype(F32) * dp
                deltas.append(delta[c] + jnp.sum(term.reshape(16, 8, 256), axis=0))
                o_sc[sel, :, cols] += mm(v, p, TN)
            return tuple(deltas)

        delta = tuple(jnp.zeros((8, 256), F32) for _ in range(4))
        delta = lax.fori_loop(0, count + 1, first, delta)
        delta = [jnp.sum(t, axis=0, keepdims=True) for t in delta]

        def second(j, none, sel=sel, base=base, delta=delta):
            k = r1_ref[j, SR + DR : SR + DR + T, :]
            acc = dk_sc[j]
            for c in range(4):
                cols = slice(c * 256, (c + 1) * 256)
                p = p_ref[base + j, :, cols].astype(F32)
                ds = (p * (dp_sc[base + j, :, cols] - delta[c])).astype(BF)
                dq_sc[sel, :, cols] += mm(k, ds, TN)
                acc = acc + mm(ds, qs_ref[sel, cols, :])
            dk_sc[j] = acc
            return none

        lax.fori_loop(0, count + 1, second, 0)

    for c in range(32):
        pay_ref[c, SR : SR + T, :] = dk_sc[c].astype(BF)
    for h in range(GH):
        o_ref[0:T, head(h)] = jnp.transpose(o_sc[upper, :, head(h)])
        o_ref[T : 2 * T, head(h)] = jnp.transpose(dq_sc[upper, :, head(h)]) * SCALE
        send_ref[0:T, head(h)] = jnp.transpose(o_sc[1 - upper, :, head(h)]).astype(BF)
        send_ref[T : 2 * T, head(h)] = (
            jnp.transpose(dq_sc[1 - upper, :, head(h)]) * SCALE
        ).astype(BF)


def final_kernel(
    x_ref, b_ref, c_ref, dt_ref, a_ref, skip_ref, dy_ref, r2_ref, r5_ref,
    gx_ref, gb_ref, gc_ref, gk_ref
):
    cum = sums_by_token(dt_ref, a_ref)
    cum_t, dt_t = sums_by_head(dt_ref, a_ref)
    grow = jnp.exp(cum)
    weight = jnp.exp(cum[T - 1 : T, :] - cum) * dt_ref[...]
    lower = lower_tri()
    for g in range(2):
        b = b_ref[:, head(g)]
        cc = c_ref[:, head(g)]
        cb = mm(cc, b, NT)
        mixed = jnp.zeros((T, T), F32)
        gb = jnp.zeros((T, T), F32)
        gc = jnp.zeros((T, T), F32)
        for h in range(g * GH, (g + 1) * GH):
            gap = cum[:, h : h + 1] - cum_t[h : h + 1, :]
            decay = jnp.exp(jnp.where(lower, gap, NEG)) * dt_t[h : h + 1, :]
            mix = (cb * decay).astype(BF)
            x = x_ref[:, head(h)]
            dy = dy_ref[:, head(h)]
            dyb = dy.astype(BF)
            enter = jnp.concatenate([r2_ref[2 * h, 0:SR, :], r2_ref[2 * h + 1, 0:SR, :]], 0)
            sg = jnp.concatenate([r5_ref[2 * h, 0:SR, :], r5_ref[2 * h + 1, 0:SR, :]], 0)
            gx = mm(mix, dyb, TN) + skip_ref[:, h : h + 1] * dy
            gx_ref[:, head(h)] = gx + weight[:, h : h + 1] * mm(b, sg, NT)
            mixed = mixed + mm(dyb, x, NT) * decay
            gb = gb + weight[:, h : h + 1] * mm(x, sg)
            gc = gc + grow[:, h : h + 1] * mm(dyb, enter)
        mixed = mixed.astype(BF)
        gb_ref[:, head(g)] = gb + mm(mixed, cc, TN)
        gc_ref[:, head(g)] = gc + mm(mixed, b)
    for k in range(2):
        acc = r5_ref[16 * k, SR : SR + T, :].astype(F32)
        for s in range(1, 16):
            acc = acc + r5_ref[16 * k + s, SR : SR + T, :].astype(F32)
        gk_ref[:, head(k)] = acc * SCALE


VM = pl.BlockSpec(memory_space=pltpu.VMEM)
SM = pl.BlockSpec(memory_space=pltpu.SMEM)


def call(kernel, outs, scratch, name, mib, flops, nbytes, *args):
    return pl.pallas_call(
        kernel,
        name=name,
        out_shape=[jax.ShapeDtypeStruct(s, d) for s, d in outs],
        in_specs=[SM if a.dtype == jnp.int32 else VM for a in args],
        out_specs=[VM] * len(outs),
        scratch_shapes=[pltpu.VMEM(s, d) for s, d in scratch],
        cost_estimate=pl.CostEstimate(
            flops=flops, bytes_accessed=nbytes, transcendentals=0
        ),
        compiler_params=pltpu.CompilerParams(vmem_limit_bytes=mib << 20),
    )(*args)


def over_ctx(pay):
    return lax.all_to_all(pay, "ctx", 0, 0, tiled=True)


def body(
    mamba_x, mamba_b, mamba_c, step_dt, decay_a, skip_d, value_weight, queries, keys, out_grad
):
    at = lax.axis_index("ctx")
    at1 = at.astype(jnp.int32).reshape(1)
    upper = at >= 16
    a_row = decay_a.reshape(1, NH)
    skip_row = skip_d.reshape(1, NH)
    swap = [(i, 31 - i) for i in range(32)]

    away = jnp.concatenate(
        [
            jnp.where(upper, queries[:, :1024], queries[:, 1024:]),
            jnp.where(upper, out_grad[:, :1024], out_grad[:, 1024:]),
        ],
        axis=0,
    )
    other = lax.ppermute(away, "ctx", swap)
    (pay1,) = call(
        state_kernel, [((32, SR + DR + T, T), BF)], [], "block_states", 24, 1 << 27, 1 << 22,
        mamba_x, mamba_b, step_dt, a_row, keys,
    )
    r1 = over_ctx(pay1)
    pay2, probs, qs, ds = call(
        probs_kernel,
        [((32, SR + T, T), BF), ((33, T, 1024), BF), ((2, 1024, T), BF), ((2, 1024, T), BF)],
        [((33, T, 1024), F32), ((32, T, T), F32)],
        "probs", 56, 1 << 32, 1 << 24, at1, r1, queries, out_grad, other,
    )
    r2 = over_ctx(pay2)
    (pay3,) = call(
        values_kernel, [((4, T, 512), BF)], [((T, 2048), BF)], "values", 32, 1 << 30, 1 << 23,
        mamba_x, mamba_b, mamba_c, step_dt, a_row, skip_row, r2, value_weight,
    )
    r3 = lax.all_to_all(pay3, ("ch", "section"), 0, 0, tiled=True)
    pay4, dy = call(
        back_kernel, [((32, SR + T, T), BF), ((T, 2048), F32)], [], "value_back", 32, 1 << 30,
        1 << 23, r3, value_weight, mamba_c, step_dt, a_row,
    )
    r4 = over_ctx(pay4)
    pay5, kept, send = call(
        grads_kernel,
        [((32, SR + T, T), BF), ((256, 1024), F32), ((256, 1024), BF)],
        [((33, T, 1024), F32), ((2, T, 1024), F32), ((2, T, 1024), F32), ((32, T, T), F32)],
        "attention_grads", 60, 1 << 32, 1 << 24, at1, r1, r4, probs, qs, ds,
    )
    back = lax.ppermute(send, "ctx", swap)
    r5 = over_ctx(pay5)
    grad_x, grad_b, grad_c, grad_k = call(
        final_kernel,
        [((T, 2048), F32), ((T, 256), F32), ((T, 256), F32), ((T, 256), F32)],
        [], "mixer_grads", 32, 1 << 29, 1 << 23,
        mamba_x, mamba_b, mamba_c, step_dt, a_row, skip_row, dy, r2, r5,
    )
    back = back.astype(F32)
    whole = jnp.where(
        upper, jnp.concatenate([back, kept], axis=1), jnp.concatenate([kept, back], axis=1)
    )
    return (whole[:T], whole[T:], grad_k, grad_x, grad_b, grad_c)


def solution(mesh):
    tokens = P("ctx", ("ch", "section"))
    heads = P(("ch", "section"))
    in_specs = (
        tokens, tokens, tokens, tokens, heads, heads, P(("ch", "section"), None),
        tokens, tokens, tokens,
    )
    return jax.shard_map(
        body, mesh=mesh, in_specs=in_specs, out_specs=(tokens,) * 6, check_vma=False
    )
```

```python
import math

import jax
import jax.numpy as jnp
from jax import lax
from jax.experimental import pallas as pl
from jax.experimental.pallas import tpu as pltpu
from jax.sharding import PartitionSpec as P

T = 128
NH = 16
GH = 8
F32 = jnp.float32
BF = jnp.bfloat16
HI = lax.Precision.HIGHEST
SCALE = 1.0 / math.sqrt(128.0)
SR = 64
DR = 16
NEG = -1e30

NN = (((1,), (0,)), ((), ()))
NT = (((1,), (1,)), ((), ()))
TN = (((0,), (0,)), ((), ()))


def mm(a, b, dims=NN):
    return lax.dot_general(a, b, dims, preferred_element_type=F32)


def mm_exact(a, b, dims=NN):
    return lax.dot_general(a, b, dims, precision=HI, preferred_element_type=F32)


def head(h):
    return slice(h * T, (h + 1) * T)


def lower_tri():
    row = lax.broadcasted_iota(jnp.int32, (T, T), 0)
    col = lax.broadcasted_iota(jnp.int32, (T, T), 1)
    return row >= col


def sums_by_token(dt_ref, a_ref):
    steps = -dt_ref[...] * a_ref[...]
    return mm_exact(lower_tri().astype(F32), steps)


def sums_by_head(dt_ref, a_ref):
    row = lax.broadcasted_iota(jnp.int32, (T, T), 0)
    col = lax.broadcasted_iota(jnp.int32, (T, T), 1)
    steps = -dt_ref[...] * a_ref[...]
    upper = (row <= col).astype(F32)
    same = (row == col).astype(F32)
    return mm_exact(steps, upper, TN), mm_exact(dt_ref[...], same, TN)


def state_kernel(x_ref, b_ref, dt_ref, a_ref, k_ref, out_ref):
    cum = sums_by_token(dt_ref, a_ref)
    total = cum[T - 1 : T, :]
    weight = jnp.exp(total - cum) * dt_ref[...]
    first = total.astype(BF).astype(F32)
    second = (total - first).astype(BF).astype(F32)
    third = total - first - second
    row = lax.broadcasted_iota(jnp.int32, (DR, T), 0)
    for h in range(NH):
        g = h // GH
        xw = (x_ref[:, head(h)].astype(F32) * weight[:, h : h + 1]).astype(BF)
        state = mm(xw, b_ref[:, head(g)], TN).astype(BF)
        parts = jnp.where(
            row == 0,
            first[:, h : h + 1],
            jnp.where(row == 1, second[:, h : h + 1], third[:, h : h + 1]),
        ).astype(BF)
        for half in range(2):
            d = 2 * h + half
            out_ref[d, 0:SR, :] = state[half * SR : (half + 1) * SR]
            out_ref[d, SR : SR + DR, :] = parts
    for d in range(32):
        out_ref[d, SR + DR : SR + DR + T, :] = k_ref[:, head(d // 16)]


def decay_of(r1_ref, c):
    parts = r1_ref[c, SR : SR + DR, :].astype(F32)
    return jnp.exp(parts[0:1] + parts[1:2] + parts[2:3])


def steps_of(n, step, init):
    whole = n // 4
    init = lax.fori_loop(0, whole, lambda i, c: step(i * 4, 4, c), init)
    pairs = (n - whole * 4) // 2
    init = lax.fori_loop(0, pairs, lambda i, c: step(whole * 4, 2, c), init)
    return lax.fori_loop(whole * 4 + pairs * 2, n, lambda i, c: step(i, 1, c), init)


def rows_of(ref, j, u, first):
    return jnp.concatenate([ref[j + n, first : first + T, :] for n in range(u)], axis=0)


def quarter(c):
    return slice(c * 256, (c + 1) * 256)


def fold(x):
    return x.reshape(-1, 8, 256)


def probs_kernel(
    at_ref, r1_ref, q_ref, d_ref, other_ref, pay_ref, p_hbm, qs_ref, ds_ref,
    s_sc, dv_sc, qt_sc, sem
):
    at = at_ref[0]
    upper = (at >= 16).astype(jnp.int32)
    low = jnp.minimum(at, 31 - at)

    for h in range(GH):
        own = pl.ds(pl.multiple_of(upper * 1024 + h * T, T), T)
        qs_ref[upper, head(h), :] = q_ref[:, own]
        ds_ref[upper, head(h), :] = d_ref[:, own]
        qs_ref[1 - upper, head(h), :] = other_ref[0:T, head(h)]
        ds_ref[1 - upper, head(h), :] = other_ref[T : 2 * T, head(h)]
        qt_sc[upper, :, head(h)] = jnp.transpose(q_ref[:, own])
        qt_sc[1 - upper, :, head(h)] = jnp.transpose(other_ref[0:T, head(h)])

    dv_sc[...] = jnp.zeros_like(dv_sc)
    key = lax.broadcasted_iota(jnp.int32, (T, 256), 0)
    tok = lax.broadcasted_iota(jnp.int32, (T, 256), 1) & (T - 1)
    seen = key <= tok

    for sel in range(2):
        count = low if sel == 0 else 31 - low
        base = 0 if sel == 0 else low + 1

        def scores(j, u, top, diag=False, sel=sel, base=base):
            k = rows_of(r1_ref, j, u, SR + DR)
            tops = []
            for c in range(4):
                s = mm(k, qt_sc[sel, :, quarter(c)])
                if diag:
                    s = jnp.where(seen, s, NEG)
                s_sc[pl.ds(base + j, u), :, quarter(c)] = s.reshape(u, T, 256)
                tops.append(jnp.maximum(top[c], jnp.max(fold(s), axis=0)))
            return tuple(tops)

        top = tuple(jnp.full((8, 256), NEG, F32) for _ in range(4))
        top = steps_of(count, scores, top)
        top = scores(count, 1, top, True)
        peak = [jnp.max(t, axis=0, keepdims=True) for t in top]

        def weigh(j, u, tot, base=base, peak=peak):
            tots = []
            for c in range(4):
                p = jnp.exp((s_sc[pl.ds(base + j, u), :, quarter(c)] - peak[c]) * SCALE)
                tots.append(tot[c] + jnp.sum(fold(p), axis=0))
            return tuple(tots)

        tot = tuple(jnp.zeros((8, 256), F32) for _ in range(4))
        tot = steps_of(count + 1, weigh, tot)
        shift = [
            peak[c] * SCALE + jnp.log(jnp.sum(tot[c], axis=0, keepdims=True)) for c in range(4)
        ]

        def spread(j, u, none, sel=sel, base=base, shift=shift):
            ps = []
            at_b = pl.ds(base + j, u)
            for c in range(4):
                p = jnp.exp(s_sc[at_b, :, quarter(c)] * SCALE - shift[c])
                s_sc[at_b, :, quarter(c)] = p
                ps.append(p.astype(BF).reshape(u * T, 256))
            term = mm(jnp.concatenate(ps, axis=1), ds_ref[sel])
            dv_sc[pl.ds(j, u)] = dv_sc[pl.ds(j, u)] + term.reshape(u, T, T)
            pltpu.make_async_copy(s_sc.at[at_b], p_hbm.at[at_b], sem).start()
            return none

        steps_of(count + 1, spread, 0)

    run = jnp.zeros((SR, T), F32)
    for c in range(32):
        pay_ref[c, 0:SR, :] = run.astype(BF)
        run = decay_of(r1_ref, c) * run + r1_ref[c, 0:SR, :].astype(F32)
    for c in range(32):
        pay_ref[c, SR : SR + T, :] = dv_sc[c].astype(BF)
    pltpu.make_async_copy(s_sc, p_hbm, sem).wait()


def split(x):
    big = x.astype(BF)
    return big, (x - big.astype(F32)).astype(BF)


def values_kernel(
    x_ref, b_ref, c_ref, dt_ref, a_ref, skip_ref, r2_ref, w_ref, out_ref, y_sc
):
    cum = sums_by_token(dt_ref, a_ref)
    cum_t, dt_t = sums_by_head(dt_ref, a_ref)
    grow = jnp.exp(cum)
    lower = lower_tri()
    for g in range(2):
        cb = mm(c_ref[:, head(g)], b_ref[:, head(g)], NT)
        for h in range(g * GH, (g + 1) * GH):
            gap = cum[:, h : h + 1] - cum_t[h : h + 1, :]
            mix = cb * jnp.exp(jnp.where(lower, gap, NEG)) * dt_t[h : h + 1, :]
            x = x_ref[:, head(h)]
            enter = jnp.concatenate([r2_ref[2 * h, 0:SR, :], r2_ref[2 * h + 1, 0:SR, :]], 0)
            mix, rest = split(mix)
            y = mm(mix, x) + mm(rest, x) + skip_ref[:, h : h + 1] * x.astype(F32)
            y = y + grow[:, h : h + 1] * mm(c_ref[:, head(g)], enter, NT)
            y_sc[:, head(h)] = y.astype(BF)
    dv = []
    for k in range(2):
        acc = r2_ref[16 * k, SR : SR + T, :].astype(F32)
        for s in range(1, 16):
            acc = acc + r2_ref[16 * k + s, SR : SR + T, :].astype(F32)
        dv.append(acc.astype(BF))
    for d in range(4):
        big, rest = split(mm(y_sc[...], w_ref[:, quarter(d)]))
        out_ref[d, :, 0:256] = big
        out_ref[d, :, 256:512] = rest
        out_ref[d, :, 512:640] = dv[0]
        out_ref[d, :, 640:768] = dv[1]


def back_kernel(r3_ref, w_ref, c_ref, dt_ref, a_ref, pay_ref, dy_ref):
    values = r3_ref[0, :, 0:256].astype(F32) + r3_ref[0, :, 256:512].astype(F32)
    for s in range(1, 4):
        values = values + r3_ref[s, :, 0:256].astype(F32)
        values = values + r3_ref[s, :, 256:512].astype(F32)
    values = values.astype(BF)
    for d in range(32):
        pay_ref[d, SR : SR + T, :] = values[:, head(d // 16)]
    vg = jnp.concatenate([r3_ref[s, :, 512:768] for s in range(4)], axis=1)
    grow = jnp.exp(sums_by_token(dt_ref, a_ref))
    for h in range(NH):
        dy = mm(vg, w_ref[head(h), :], NT)
        dy_ref[:, head(h)] = dy
        eg = mm((dy * grow[:, h : h + 1]).astype(BF), c_ref[:, head(h // GH)], TN).astype(BF)
        pay_ref[2 * h, 0:SR, :] = eg[0:SR]
        pay_ref[2 * h + 1, 0:SR, :] = eg[SR:T]


def grads_kernel(
    at_ref, r1_ref, r4_ref, qs_ref, ds_ref, p_hbm, pay_ref, o_ref, send_ref,
    p_sc, dp_sc, o_sc, dq_sc, dk_sc, dt_sc, sem
):
    at = at_ref[0]
    upper = (at >= 16).astype(jnp.int32)
    low = jnp.minimum(at, 31 - at)
    for b in range(33):
        pltpu.make_async_copy(p_hbm.at[b], p_sc.at[b], sem.at[b]).start()

    run = jnp.zeros((SR, T), F32)
    for c in range(31, -1, -1):
        pay_ref[c, 0:SR, :] = run.astype(BF)
        run = decay_of(r1_ref, c) * run + r4_ref[c, 0:SR, :].astype(F32)

    for sel in range(2):
        for h in range(GH):
            dt_sc[sel, :, head(h)] = jnp.transpose(ds_ref[sel, head(h), :])
    dk_sc[...] = jnp.zeros_like(dk_sc)
    o_sc[...] = jnp.zeros_like(o_sc)
    dq_sc[...] = jnp.zeros_like(dq_sc)
    for sel in range(2):
        count = low if sel == 0 else 31 - low
        base = 0 if sel == 0 else low + 1

        def first(j, u, delta, sel=sel, base=base):
            for n in range(u):
                b = base + j + n
                pltpu.make_async_copy(p_hbm.at[b], p_sc.at[b], sem.at[b]).wait()
            at_b = pl.ds(base + j, u)
            v = rows_of(r4_ref, j, u, SR)
            v_t = jnp.transpose(v)
            deltas = []
            for c in range(4):
                p = p_sc[at_b, :, quarter(c)].astype(BF).reshape(u * T, 256)
                dp = mm(v, dt_sc[sel, :, quarter(c)])
                dp_sc[at_b, :, quarter(c)] = dp.reshape(u, T, 256)
                term = p.astype(F32) * dp
                deltas.append(delta[c] + jnp.sum(fold(term), axis=0))
                o_sc[sel, :, quarter(c)] += mm(v_t, p)
            return tuple(deltas)

        delta = tuple(jnp.zeros((8, 256), F32) for _ in range(4))
        delta = steps_of(count + 1, first, delta)
        delta = [jnp.sum(t, axis=0, keepdims=True) for t in delta]

        def second(j, u, none, sel=sel, base=base, delta=delta):
            at_b = pl.ds(base + j, u)
            k_t = jnp.transpose(rows_of(r1_ref, j, u, SR + DR))
            parts = []
            for c in range(4):
                ds = p_sc[at_b, :, quarter(c)] * (dp_sc[at_b, :, quarter(c)] - delta[c])
                ds = ds.astype(BF).reshape(u * T, 256)
                dq_sc[sel, :, quarter(c)] += mm(k_t, ds)
                parts.append(ds)
            term = mm(jnp.concatenate(parts, axis=1), qs_ref[sel])
            dk_sc[pl.ds(j, u)] = dk_sc[pl.ds(j, u)] + term.reshape(u, T, T)
            return none

        steps_of(count + 1, second, 0)

    for c in range(32):
        pay_ref[c, SR : SR + T, :] = dk_sc[c].astype(BF)
    for h in range(GH):
        o_ref[0:T, head(h)] = jnp.transpose(o_sc[upper, :, head(h)])
        o_ref[T : 2 * T, head(h)] = jnp.transpose(dq_sc[upper, :, head(h)]) * SCALE
        send_ref[0:T, head(h)] = jnp.transpose(o_sc[1 - upper, :, head(h)]).astype(BF)
        send_ref[T : 2 * T, head(h)] = (
            jnp.transpose(dq_sc[1 - upper, :, head(h)]) * SCALE
        ).astype(BF)


def local_kernel(
    x_ref, b_ref, c_ref, dt_ref, a_ref, skip_ref, dy_ref, r2_ref, gx_ref, gb_ref, gc_ref
):
    cum = sums_by_token(dt_ref, a_ref)
    cum_t, dt_t = sums_by_head(dt_ref, a_ref)
    grow = jnp.exp(cum)
    lower = lower_tri()
    for g in range(2):
        b = b_ref[:, head(g)]
        cc = c_ref[:, head(g)]
        cb = mm(cc, b, NT)
        mixed = jnp.zeros((T, T), F32)
        gc = jnp.zeros((T, T), F32)
        for h in range(g * GH, (g + 1) * GH):
            gap = cum[:, h : h + 1] - cum_t[h : h + 1, :]
            decay = jnp.exp(jnp.where(lower, gap, NEG)) * dt_t[h : h + 1, :]
            mix = (cb * decay).astype(BF)
            x = x_ref[:, head(h)]
            dy = dy_ref[:, head(h)]
            dyb = dy.astype(BF)
            enter = jnp.concatenate([r2_ref[2 * h, 0:SR, :], r2_ref[2 * h + 1, 0:SR, :]], 0)
            gx_ref[:, head(h)] = mm(mix, dyb, TN) + skip_ref[:, h : h + 1] * dy
            mixed = mixed + mm(dyb, x, NT) * decay
            gc = gc + grow[:, h : h + 1] * mm(dyb, enter)
        mixed = mixed.astype(BF)
        gb_ref[:, head(g)] = mm(mixed, cc, TN)
        gc_ref[:, head(g)] = gc + mm(mixed, b)


def final_kernel(
    x_ref, b_ref, dt_ref, a_ref, gx0_ref, gb0_ref, r5_ref, gx_ref, gb_ref, gk_ref
):
    cum = sums_by_token(dt_ref, a_ref)
    weight = jnp.exp(cum[T - 1 : T, :] - cum) * dt_ref[...]
    for g in range(2):
        b = b_ref[:, head(g)]
        gb = gb0_ref[:, head(g)]
        for h in range(g * GH, (g + 1) * GH):
            sg = jnp.concatenate([r5_ref[2 * h, 0:SR, :], r5_ref[2 * h + 1, 0:SR, :]], 0)
            gx_ref[:, head(h)] = gx0_ref[:, head(h)] + weight[:, h : h + 1] * mm(b, sg, NT)
            gb = gb + weight[:, h : h + 1] * mm(x_ref[:, head(h)], sg)
        gb_ref[:, head(g)] = gb
    for k in range(2):
        acc = r5_ref[16 * k, SR : SR + T, :].astype(F32)
        for s in range(1, 16):
            acc = acc + r5_ref[16 * k + s, SR : SR + T, :].astype(F32)
        gk_ref[:, head(k)] = acc * SCALE


VM = pl.BlockSpec(memory_space=pltpu.VMEM)
SM = pl.BlockSpec(memory_space=pltpu.SMEM)
ANY = pl.BlockSpec(memory_space=pl.ANY)


def call(kernel, outs, scratch, name, mib, flops, nbytes, *args, far_in=(), far_out=()):
    places = [SM if a.dtype == jnp.int32 else VM for a in args]
    return pl.pallas_call(
        kernel,
        name=name,
        out_shape=[jax.ShapeDtypeStruct(s, d) for s, d in outs],
        in_specs=[ANY if n in far_in else place for n, place in enumerate(places)],
        out_specs=[ANY if n in far_out else VM for n in range(len(outs))],
        scratch_shapes=scratch,
        cost_estimate=pl.CostEstimate(
            flops=flops, bytes_accessed=nbytes, transcendentals=0
        ),
        compiler_params=pltpu.CompilerParams(vmem_limit_bytes=mib << 20),
    )(*args)


def over_ctx(pay):
    return lax.all_to_all(pay, "ctx", 0, 0, tiled=True)


def body(
    mamba_x, mamba_b, mamba_c, step_dt, decay_a, skip_d, value_weight, queries, keys, out_grad
):
    at = lax.axis_index("ctx")
    at1 = at.astype(jnp.int32).reshape(1)
    upper = at >= 16
    a_row = decay_a.reshape(1, NH)
    skip_row = skip_d.reshape(1, NH)
    swap = [(i, 31 - i) for i in range(32)]

    away = jnp.concatenate(
        [
            jnp.where(upper, queries[:, :1024], queries[:, 1024:]),
            jnp.where(upper, out_grad[:, :1024], out_grad[:, 1024:]),
        ],
        axis=0,
    )
    other = lax.ppermute(away, "ctx", swap)
    (pay1,) = call(
        state_kernel, [((32, SR + DR + T, T), BF)], [], "block_states", 24, 1 << 27, 1 << 22,
        mamba_x, mamba_b, step_dt, a_row, keys,
    )
    r1 = over_ctx(pay1)
    pay2, probs, qs, ds = call(
        probs_kernel,
        [((32, SR + T, T), BF), ((33, T, 1024), F32), ((2, 1024, T), BF), ((2, 1024, T), BF)],
        [
            pltpu.VMEM((33, T, 1024), F32), pltpu.VMEM((32, T, T), F32),
            pltpu.VMEM((2, T, 1024), BF), pltpu.SemaphoreType.DMA,
        ],
        "probs", 40, 1 << 32, 1 << 25, at1, r1, queries, out_grad, other, far_out=(1,),
    )
    r2 = over_ctx(pay2)
    (pay3,) = call(
        values_kernel, [((4, T, 768), BF)], [pltpu.VMEM((T, 2048), BF)], "values", 24,
        1 << 30, 1 << 23,
        mamba_x, mamba_b, mamba_c, step_dt, a_row, skip_row, r2, value_weight,
    )
    r3 = lax.all_to_all(pay3, ("ch", "section"), 0, 0, tiled=True)
    pay4, dy = call(
        back_kernel, [((32, SR + T, T), BF), ((T, 2048), F32)], [], "value_back", 24, 1 << 30,
        1 << 23, r3, value_weight, mamba_c, step_dt, a_row,
    )
    r4 = over_ctx(pay4)
    gx0, gb0, grad_c = call(
        local_kernel,
        [((T, 2048), F32), ((T, 256), F32), ((T, 256), F32)], [], "mixer_local", 24,
        1 << 29, 1 << 23,
        mamba_x, mamba_b, mamba_c, step_dt, a_row, skip_row, dy, r2,
    )
    pay5, kept, send = call(
        grads_kernel,
        [((32, SR + T, T), BF), ((256, 1024), F32), ((256, 1024), BF)],
        [
            pltpu.VMEM((33, T, 1024), F32), pltpu.VMEM((33, T, 1024), F32),
            pltpu.VMEM((2, T, 1024), F32), pltpu.VMEM((2, T, 1024), F32),
            pltpu.VMEM((32, T, T), F32), pltpu.VMEM((2, T, 1024), BF),
            pltpu.SemaphoreType.DMA((33,)),
        ],
        "attention_grads", 56, 1 << 32, 1 << 25, at1, r1, r4, qs, ds, probs, far_in=(5,),
    )
    back = lax.ppermute(send, "ctx", swap)
    r5 = over_ctx(pay5)
    grad_x, grad_b, grad_k = call(
        final_kernel,
        [((T, 2048), F32), ((T, 256), F32), ((T, 256), F32)],
        [], "mixer_grads", 24, 1 << 29, 1 << 23,
        mamba_x, mamba_b, step_dt, a_row, gx0, gb0, r5,
    )
    back = back.astype(F32)
    whole = jnp.where(
        upper, jnp.concatenate([back, kept], axis=1), jnp.concatenate([kept, back], axis=1)
    )
    return (whole[:T], whole[T:], grad_k, grad_x, grad_b, grad_c)


def solution(mesh):
    tokens = P("ctx", ("ch", "section"))
    heads = P(("ch", "section"))
    in_specs = (
        tokens, tokens, tokens, tokens, heads, heads, P(("ch", "section"), None),
        tokens, tokens, tokens,
    )
    return jax.shard_map(
        body, mesh=mesh, in_specs=in_specs, out_specs=(tokens,) * 6, check_vma=False
    )
```

```python
import math

import jax
import jax.numpy as jnp
from jax import lax
from jax.experimental import pallas as pl
from jax.experimental.pallas import tpu as pltpu
from jax.sharding import PartitionSpec as P

T = 128
NH = 16
GH = 8
F32 = jnp.float32
BF = jnp.bfloat16
HI = lax.Precision.HIGHEST
SCALE = 1.0 / math.sqrt(128.0)
SR = 64
DR = 16
NEG = -1e30

NN = (((1,), (0,)), ((), ()))
NT = (((1,), (1,)), ((), ()))
TN = (((0,), (0,)), ((), ()))


def mm(a, b, dims=NN):
    return lax.dot_general(a, b, dims, preferred_element_type=F32)


def mm_exact(a, b, dims=NN):
    return lax.dot_general(a, b, dims, precision=HI, preferred_element_type=F32)


def head(h):
    return slice(h * T, (h + 1) * T)


def lower_tri():
    row = lax.broadcasted_iota(jnp.int32, (T, T), 0)
    col = lax.broadcasted_iota(jnp.int32, (T, T), 1)
    return row >= col


def sums_by_token(dt_ref, a_ref):
    steps = -dt_ref[...] * a_ref[...]
    return mm_exact(lower_tri().astype(F32), steps)


def sums_by_head(dt_ref, a_ref):
    row = lax.broadcasted_iota(jnp.int32, (T, T), 0)
    col = lax.broadcasted_iota(jnp.int32, (T, T), 1)
    steps = -dt_ref[...] * a_ref[...]
    upper = (row <= col).astype(F32)
    same = (row == col).astype(F32)
    return mm_exact(steps, upper, TN), mm_exact(dt_ref[...], same, TN)


def state_kernel(x_ref, b_ref, dt_ref, a_ref, k_ref, out_ref):
    cum = sums_by_token(dt_ref, a_ref)
    total = cum[T - 1 : T, :]
    weight = jnp.exp(total - cum) * dt_ref[...]
    first = total.astype(BF).astype(F32)
    second = (total - first).astype(BF).astype(F32)
    third = total - first - second
    row = lax.broadcasted_iota(jnp.int32, (DR, T), 0)
    for h in range(NH):
        g = h // GH
        xw = (x_ref[:, head(h)].astype(F32) * weight[:, h : h + 1]).astype(BF)
        state = mm(xw, b_ref[:, head(g)], TN).astype(BF)
        parts = jnp.where(
            row == 0,
            first[:, h : h + 1],
            jnp.where(row == 1, second[:, h : h + 1], third[:, h : h + 1]),
        ).astype(BF)
        for half in range(2):
            d = 2 * h + half
            out_ref[d, 0:SR, :] = state[half * SR : (half + 1) * SR]
            out_ref[d, SR : SR + DR, :] = parts
    for d in range(32):
        out_ref[d, SR + DR : SR + DR + T, :] = k_ref[:, head(d // 16)]


def decay_of(r1_ref, c):
    parts = r1_ref[c, SR : SR + DR, :].astype(F32)
    return jnp.exp(parts[0:1] + parts[1:2] + parts[2:3])


def steps_of(n, step, init):
    whole = n // 4
    init = lax.fori_loop(0, whole, lambda i, c: step(i * 4, 4, c), init)
    pairs = (n - whole * 4) // 2
    init = lax.fori_loop(0, pairs, lambda i, c: step(whole * 4, 2, c), init)
    return lax.fori_loop(whole * 4 + pairs * 2, n, lambda i, c: step(i, 1, c), init)


def rows_of(ref, j, u, first):
    return jnp.concatenate([ref[j + n, first : first + T, :] for n in range(u)], axis=0)


def quarter(c):
    return slice(c * 256, (c + 1) * 256)


def fold(x):
    return x.reshape(-1, 8, 256)


def probs_kernel(
    at_ref, r1_ref, q_ref, d_ref, other_ref, pay_ref, p_hbm, qs_ref, ds_ref,
    s_sc, dv_sc, qt_sc, sem
):
    at = at_ref[0]
    upper = (at >= 16).astype(jnp.int32)
    low = jnp.minimum(at, 31 - at)

    for h in range(GH):
        own = pl.ds(pl.multiple_of(upper * 1024 + h * T, T), T)
        qs_ref[upper, head(h), :] = q_ref[:, own]
        ds_ref[upper, head(h), :] = d_ref[:, own]
        qs_ref[1 - upper, head(h), :] = other_ref[0:T, head(h)]
        ds_ref[1 - upper, head(h), :] = other_ref[T : 2 * T, head(h)]
        qt_sc[upper, :, head(h)] = jnp.transpose(q_ref[:, own])
        qt_sc[1 - upper, :, head(h)] = jnp.transpose(other_ref[0:T, head(h)])

    dv_sc[...] = jnp.zeros_like(dv_sc)
    key = lax.broadcasted_iota(jnp.int32, (T, 256), 0)
    tok = lax.broadcasted_iota(jnp.int32, (T, 256), 1) & (T - 1)
    seen = key <= tok

    for sel in range(2):
        count = low if sel == 0 else 31 - low
        base = 0 if sel == 0 else low + 1

        def scores(j, u, top, diag=False, sel=sel, base=base):
            k = rows_of(r1_ref, j, u, SR + DR)
            tops = []
            for c in range(4):
                s = mm(k, qt_sc[sel, :, quarter(c)])
                if diag:
                    s = jnp.where(seen, s, NEG)
                s_sc[pl.ds(base + j, u), :, quarter(c)] = s.reshape(u, T, 256)
                tops.append(jnp.maximum(top[c], jnp.max(fold(s), axis=0)))
            return tuple(tops)

        top = tuple(jnp.full((8, 256), NEG, F32) for _ in range(4))
        top = steps_of(count, scores, top)
        top = scores(count, 1, top, True)
        peak = [jnp.max(t, axis=0, keepdims=True) for t in top]

        def weigh(j, u, tot, base=base, peak=peak):
            tots = []
            for c in range(4):
                p = jnp.exp((s_sc[pl.ds(base + j, u), :, quarter(c)] - peak[c]) * SCALE)
                tots.append(tot[c] + jnp.sum(fold(p), axis=0))
            return tuple(tots)

        tot = tuple(jnp.zeros((8, 256), F32) for _ in range(4))
        tot = steps_of(count + 1, weigh, tot)
        shift = [
            peak[c] * SCALE + jnp.log(jnp.sum(tot[c], axis=0, keepdims=True)) for c in range(4)
        ]

        def spread(j, u, none, sel=sel, base=base, shift=shift):
            ps = []
            at_b = pl.ds(base + j, u)
            for c in range(4):
                p = jnp.exp(s_sc[at_b, :, quarter(c)] * SCALE - shift[c])
                s_sc[at_b, :, quarter(c)] = p
                ps.append(p.astype(BF).reshape(u * T, 256))
            term = mm(jnp.concatenate(ps, axis=1), ds_ref[sel])
            dv_sc[pl.ds(j, u)] = dv_sc[pl.ds(j, u)] + term.reshape(u, T, T)
            pltpu.make_async_copy(s_sc.at[at_b], p_hbm.at[at_b], sem).start()
            return none

        steps_of(count + 1, spread, 0)

    run = jnp.zeros((SR, T), F32)
    for c in range(32):
        pay_ref[c, 0:SR, :] = run.astype(BF)
        run = decay_of(r1_ref, c) * run + r1_ref[c, 0:SR, :].astype(F32)
    for c in range(32):
        pay_ref[c, SR : SR + T, :] = dv_sc[c].astype(BF)
    pltpu.make_async_copy(s_sc, p_hbm, sem).wait()


def split(x):
    big = x.astype(BF)
    return big, (x - big.astype(F32)).astype(BF)


def values_kernel(
    x_ref, b_ref, c_ref, dt_ref, a_ref, skip_ref, r2_ref, w_ref, out_ref, y_sc
):
    cum = sums_by_token(dt_ref, a_ref)
    cum_t, dt_t = sums_by_head(dt_ref, a_ref)
    grow = jnp.exp(cum)
    lower = lower_tri()
    for g in range(2):
        cb = mm(c_ref[:, head(g)], b_ref[:, head(g)], NT)
        for h in range(g * GH, (g + 1) * GH):
            gap = cum[:, h : h + 1] - cum_t[h : h + 1, :]
            mix = cb * jnp.exp(jnp.where(lower, gap, NEG)) * dt_t[h : h + 1, :]
            x = x_ref[:, head(h)]
            enter = jnp.concatenate([r2_ref[2 * h, 0:SR, :], r2_ref[2 * h + 1, 0:SR, :]], 0)
            mix, rest = split(mix)
            y = mm(mix, x) + mm(rest, x) + skip_ref[:, h : h + 1] * x.astype(F32)
            y = y + grow[:, h : h + 1] * mm(c_ref[:, head(g)], enter, NT)
            y_sc[:, head(h)] = y.astype(BF)
    dv = []
    for k in range(2):
        acc = r2_ref[16 * k, SR : SR + T, :].astype(F32)
        for s in range(1, 16):
            acc = acc + r2_ref[16 * k + s, SR : SR + T, :].astype(F32)
        dv.append(acc.astype(BF))
    for d in range(4):
        out_ref[d, :, 0:256] = mm(y_sc[...], w_ref[:, quarter(d)]).astype(BF)
        out_ref[d, :, 256:384] = dv[0]
        out_ref[d, :, 384:512] = dv[1]


def back_kernel(r3_ref, w_ref, c_ref, dt_ref, a_ref, pay_ref, dy_ref):
    values = r3_ref[0, :, 0:256].astype(F32)
    for s in range(1, 4):
        values = values + r3_ref[s, :, 0:256].astype(F32)
    values = values.astype(BF)
    for d in range(32):
        pay_ref[d, SR : SR + T, :] = values[:, head(d // 16)]
    vg = jnp.concatenate([r3_ref[s, :, 256:512] for s in range(4)], axis=1)
    grow = jnp.exp(sums_by_token(dt_ref, a_ref))
    for pair in range(NH // 2):
        both = mm(vg, w_ref[quarter(pair), :], NT)
        dy_ref[:, quarter(pair)] = both
        for n in range(2):
            h = 2 * pair + n
            grown = (both[:, head(n)] * grow[:, h : h + 1]).astype(BF)
            eg = mm(grown, c_ref[:, head(h // GH)], TN).astype(BF)
            pay_ref[2 * h, 0:SR, :] = eg[0:SR]
            pay_ref[2 * h + 1, 0:SR, :] = eg[SR:T]


def grads_kernel(
    at_ref, r1_ref, r4_ref, qs_ref, ds_ref, p_hbm, pay_ref, o_ref, send_ref,
    p_sc, dp_sc, o_sc, dq_sc, dk_sc, dt_sc, sem
):
    at = at_ref[0]
    upper = (at >= 16).astype(jnp.int32)
    low = jnp.minimum(at, 31 - at)
    for b in range(33):
        pltpu.make_async_copy(p_hbm.at[b], p_sc.at[b], sem.at[b]).start()

    run = jnp.zeros((SR, T), F32)
    for c in range(31, -1, -1):
        pay_ref[c, 0:SR, :] = run.astype(BF)
        run = decay_of(r1_ref, c) * run + r4_ref[c, 0:SR, :].astype(F32)

    for sel in range(2):
        for h in range(GH):
            dt_sc[sel, :, head(h)] = jnp.transpose(ds_ref[sel, head(h), :])
    dk_sc[...] = jnp.zeros_like(dk_sc)
    o_sc[...] = jnp.zeros_like(o_sc)
    dq_sc[...] = jnp.zeros_like(dq_sc)
    for sel in range(2):
        count = low if sel == 0 else 31 - low
        base = 0 if sel == 0 else low + 1

        def first(j, u, delta, sel=sel, base=base):
            for n in range(u):
                b = base + j + n
                pltpu.make_async_copy(p_hbm.at[b], p_sc.at[b], sem.at[b]).wait()
            at_b = pl.ds(base + j, u)
            v = rows_of(r4_ref, j, u, SR)
            v_t = jnp.transpose(v)
            deltas = []
            for c in range(4):
                p = p_sc[at_b, :, quarter(c)].astype(BF).reshape(u * T, 256)
                dp = mm(v, dt_sc[sel, :, quarter(c)])
                dp_sc[at_b, :, quarter(c)] = dp.reshape(u, T, 256)
                term = p.astype(F32) * dp
                deltas.append(delta[c] + jnp.sum(fold(term), axis=0))
                o_sc[sel, :, quarter(c)] += mm(v_t, p)
            return tuple(deltas)

        delta = tuple(jnp.zeros((8, 256), F32) for _ in range(4))
        delta = steps_of(count + 1, first, delta)
        delta = [jnp.sum(t, axis=0, keepdims=True) for t in delta]

        def second(j, u, none, sel=sel, base=base, delta=delta):
            at_b = pl.ds(base + j, u)
            k_t = jnp.transpose(rows_of(r1_ref, j, u, SR + DR))
            parts = []
            for c in range(4):
                ds = p_sc[at_b, :, quarter(c)] * (dp_sc[at_b, :, quarter(c)] - delta[c])
                ds = ds.astype(BF).reshape(u * T, 256)
                dq_sc[sel, :, quarter(c)] += mm(k_t, ds)
                parts.append(ds)
            term = mm(jnp.concatenate(parts, axis=1), qs_ref[sel])
            dk_sc[pl.ds(j, u)] = dk_sc[pl.ds(j, u)] + term.reshape(u, T, T)
            return none

        steps_of(count + 1, second, 0)

    for c in range(32):
        pay_ref[c, SR : SR + T, :] = dk_sc[c].astype(BF)
    for h in range(GH):
        o_ref[0:T, head(h)] = jnp.transpose(o_sc[upper, :, head(h)])
        o_ref[T : 2 * T, head(h)] = jnp.transpose(dq_sc[upper, :, head(h)]) * SCALE
        send_ref[0:T, head(h)] = jnp.transpose(o_sc[1 - upper, :, head(h)]).astype(BF)
        send_ref[T : 2 * T, head(h)] = (
            jnp.transpose(dq_sc[1 - upper, :, head(h)]) * SCALE
        ).astype(BF)


def local_kernel(
    x_ref, b_ref, c_ref, dt_ref, a_ref, skip_ref, dy_ref, r2_ref, gx_ref, gb_ref, gc_ref
):
    cum = sums_by_token(dt_ref, a_ref)
    cum_t, dt_t = sums_by_head(dt_ref, a_ref)
    grow = jnp.exp(cum)
    lower = lower_tri()
    for g in range(2):
        b = b_ref[:, head(g)]
        cc = c_ref[:, head(g)]
        cb = mm(cc, b, NT)
        mixed = jnp.zeros((T, T), F32)
        gc = jnp.zeros((T, T), F32)
        for h in range(g * GH, (g + 1) * GH):
            gap = cum[:, h : h + 1] - cum_t[h : h + 1, :]
            decay = jnp.exp(jnp.where(lower, gap, NEG)) * dt_t[h : h + 1, :]
            mix = (cb * decay).astype(BF)
            x = x_ref[:, head(h)]
            dy = dy_ref[:, head(h)]
            dyb = dy.astype(BF)
            enter = jnp.concatenate([r2_ref[2 * h, 0:SR, :], r2_ref[2 * h + 1, 0:SR, :]], 0)
            gx_ref[:, head(h)] = mm(mix, dyb, TN) + skip_ref[:, h : h + 1] * dy
            mixed = mixed + mm(dyb, x, NT) * decay
            gc = gc + grow[:, h : h + 1] * mm(dyb, enter)
        mixed = mixed.astype(BF)
        gb_ref[:, head(g)] = mm(mixed, cc, TN)
        gc_ref[:, head(g)] = gc + mm(mixed, b)


def final_kernel(
    x_ref, b_ref, dt_ref, a_ref, gx0_ref, gb0_ref, r5_ref, gx_ref, gb_ref, gk_ref
):
    cum = sums_by_token(dt_ref, a_ref)
    weight = jnp.exp(cum[T - 1 : T, :] - cum) * dt_ref[...]
    for g in range(2):
        b = b_ref[:, head(g)]
        gb = gb0_ref[:, head(g)]
        for h in range(g * GH, (g + 1) * GH):
            sg = jnp.concatenate([r5_ref[2 * h, 0:SR, :], r5_ref[2 * h + 1, 0:SR, :]], 0)
            gx_ref[:, head(h)] = gx0_ref[:, head(h)] + weight[:, h : h + 1] * mm(b, sg, NT)
            gb = gb + weight[:, h : h + 1] * mm(x_ref[:, head(h)], sg)
        gb_ref[:, head(g)] = gb
    for k in range(2):
        acc = r5_ref[16 * k, SR : SR + T, :].astype(F32)
        for s in range(1, 16):
            acc = acc + r5_ref[16 * k + s, SR : SR + T, :].astype(F32)
        gk_ref[:, head(k)] = acc * SCALE


VM = pl.BlockSpec(memory_space=pltpu.VMEM)
SM = pl.BlockSpec(memory_space=pltpu.SMEM)
ANY = pl.BlockSpec(memory_space=pl.ANY)


def call(kernel, outs, scratch, name, mib, flops, nbytes, *args, far_in=(), far_out=()):
    places = [SM if a.dtype == jnp.int32 else VM for a in args]
    return pl.pallas_call(
        kernel,
        name=name,
        out_shape=[jax.ShapeDtypeStruct(s, d) for s, d in outs],
        in_specs=[ANY if n in far_in else place for n, place in enumerate(places)],
        out_specs=[ANY if n in far_out else VM for n in range(len(outs))],
        scratch_shapes=scratch,
        cost_estimate=pl.CostEstimate(
            flops=flops, bytes_accessed=nbytes, transcendentals=0
        ),
        compiler_params=pltpu.CompilerParams(vmem_limit_bytes=mib << 20),
    )(*args)


def over_ctx(pay):
    return lax.all_to_all(pay, "ctx", 0, 0, tiled=True)


def body(
    mamba_x, mamba_b, mamba_c, step_dt, decay_a, skip_d, value_weight, queries, keys, out_grad
):
    at = lax.axis_index("ctx")
    at1 = at.astype(jnp.int32).reshape(1)
    upper = at >= 16
    a_row = decay_a.reshape(1, NH)
    skip_row = skip_d.reshape(1, NH)
    swap = [(i, 31 - i) for i in range(32)]

    away = jnp.concatenate(
        [
            jnp.where(upper, queries[:, :1024], queries[:, 1024:]),
            jnp.where(upper, out_grad[:, :1024], out_grad[:, 1024:]),
        ],
        axis=0,
    )
    other = lax.ppermute(away, "ctx", swap)
    (pay1,) = call(
        state_kernel, [((32, SR + DR + T, T), BF)], [], "block_states", 62, 1 << 34, 1 << 22,
        mamba_x, mamba_b, step_dt, a_row, keys,
    )
    r1 = over_ctx(pay1)
    pay2, probs, qs, ds = call(
        probs_kernel,
        [((32, SR + T, T), BF), ((33, T, 1024), F32), ((2, 1024, T), BF), ((2, 1024, T), BF)],
        [
            pltpu.VMEM((33, T, 1024), F32), pltpu.VMEM((32, T, T), F32),
            pltpu.VMEM((2, T, 1024), BF), pltpu.SemaphoreType.DMA,
        ],
        "probs", 40, 1 << 32, 1 << 25, at1, r1, queries, out_grad, other, far_out=(1,),
    )
    r2 = over_ctx(pay2)
    (pay3,) = call(
        values_kernel, [((4, T, 512), BF)], [pltpu.VMEM((T, 2048), BF)], "values", 24,
        1 << 30, 1 << 23,
        mamba_x, mamba_b, mamba_c, step_dt, a_row, skip_row, r2, value_weight,
    )
    r3 = lax.all_to_all(pay3, ("ch", "section"), 0, 0, tiled=True)
    pay4, dy = call(
        back_kernel, [((32, SR + T, T), BF), ((T, 2048), F32)], [], "value_back", 24, 1 << 30,
        1 << 23, r3, value_weight, mamba_c, step_dt, a_row,
    )
    r4 = over_ctx(pay4)
    gx0, gb0, grad_c = call(
        local_kernel,
        [((T, 2048), F32), ((T, 256), F32), ((T, 256), F32)], [], "mixer_local", 24,
        1 << 29, 1 << 23,
        mamba_x, mamba_b, mamba_c, step_dt, a_row, skip_row, dy, r2,
    )
    pay5, kept, send = call(
        grads_kernel,
        [((32, SR + T, T), BF), ((256, 1024), F32), ((256, 1024), BF)],
        [
            pltpu.VMEM((33, T, 1024), F32), pltpu.VMEM((33, T, 1024), F32),
            pltpu.VMEM((2, T, 1024), F32), pltpu.VMEM((2, T, 1024), F32),
            pltpu.VMEM((32, T, T), F32), pltpu.VMEM((2, T, 1024), BF),
            pltpu.SemaphoreType.DMA((33,)),
        ],
        "attention_grads", 56, 1 << 32, 1 << 25, at1, r1, r4, qs, ds, probs, far_in=(5,),
    )
    back = lax.ppermute(send, "ctx", swap)
    r5 = over_ctx(pay5)
    grad_x, grad_b, grad_k = call(
        final_kernel,
        [((T, 2048), F32), ((T, 256), F32), ((T, 256), F32)],
        [], "mixer_grads", 24, 1 << 29, 1 << 23,
        mamba_x, mamba_b, step_dt, a_row, gx0, gb0, r5,
    )
    back = back.astype(F32)
    whole = jnp.where(
        upper, jnp.concatenate([back, kept], axis=1), jnp.concatenate([kept, back], axis=1)
    )
    return (whole[:T], whole[T:], grad_k, grad_x, grad_b, grad_c)


def solution(mesh):
    tokens = P("ctx", ("ch", "section"))
    heads = P(("ch", "section"))
    in_specs = (
        tokens, tokens, tokens, tokens, heads, heads, P(("ch", "section"), None),
        tokens, tokens, tokens,
    )
    return jax.shard_map(
        body, mesh=mesh, in_specs=in_specs, out_specs=(tokens,) * 6, check_vma=False
    )
```

```python
import math

import jax
import jax.numpy as jnp
from jax import lax
from jax.experimental import pallas as pl
from jax.experimental.pallas import tpu as pltpu
from jax.sharding import PartitionSpec as P

T = 128
NH = 16
GH = 8
F32 = jnp.float32
BF = jnp.bfloat16
HI = lax.Precision.HIGHEST
SCALE = 1.0 / math.sqrt(128.0)
SR = 64
DR = 16
NEG = -1e30
NB = 40

NN = (((1,), (0,)), ((), ()))
NT = (((1,), (1,)), ((), ()))
TN = (((0,), (0,)), ((), ()))


def mm(a, b, dims=NN):
    return lax.dot_general(a, b, dims, preferred_element_type=F32)


def mm_exact(a, b, dims=NN):
    return lax.dot_general(a, b, dims, precision=HI, preferred_element_type=F32)


def head(h):
    return slice(h * T, (h + 1) * T)


def lower_tri():
    row = lax.broadcasted_iota(jnp.int32, (T, T), 0)
    col = lax.broadcasted_iota(jnp.int32, (T, T), 1)
    return row >= col


def same_token():
    row = lax.broadcasted_iota(jnp.int32, (T, T), 0)
    col = lax.broadcasted_iota(jnp.int32, (T, T), 1)
    return (row == col).astype(F32)


def sums_by_token(dt_ref, a_ref):
    return -mm_exact(lower_tri().astype(F32), dt_ref[...], NT) * a_ref[...]


def steps_by_token(dt_ref):
    return mm_exact(same_token(), dt_ref[...], NT)


def sums_by_head(cum):
    return mm_exact(cum, same_token(), TN)


def state_kernel(x_ref, b_ref, dt_ref, a_ref, k_ref, out_ref):
    cum = sums_by_token(dt_ref, a_ref)
    total = cum[T - 1 : T, :]
    weight = jnp.exp(total - cum) * steps_by_token(dt_ref)
    first = total.astype(BF).astype(F32)
    second = (total - first).astype(BF).astype(F32)
    third = total - first - second
    row = lax.broadcasted_iota(jnp.int32, (DR, T), 0)
    for h in range(NH):
        g = h // GH
        xw = (x_ref[:, head(h)].astype(F32) * weight[:, h : h + 1]).astype(BF)
        state = mm(xw, b_ref[:, head(g)], TN).astype(BF)
        parts = jnp.where(
            row == 0,
            first[:, h : h + 1],
            jnp.where(row == 1, second[:, h : h + 1], third[:, h : h + 1]),
        ).astype(BF)
        for half in range(2):
            d = 2 * h + half
            out_ref[d, 0:SR, :] = state[half * SR : (half + 1) * SR]
            out_ref[d, SR : SR + DR, :] = parts
    for d in range(32):
        out_ref[d, SR + DR : SR + DR + T, :] = k_ref[:, head(d // 16)]


def partner_of(at):
    return at + 24 - 16 * (at // 8)


def decay_of(r1_ref, c):
    parts = r1_ref[c, SR : SR + DR, :].astype(F32)
    return jnp.exp(parts[0:1] + parts[1:2] + parts[2:3])


def steps_of(n, step, init):
    at = 0
    for size in (8, 4, 2, 1):
        whole = (n - at) // size
        init = lax.fori_loop(
            0, whole, lambda i, c, at=at, size=size: step(at + i * size, size, c), init
        )
        at = at + whole * size
    return init


def rows_of(ref, j, u, first):
    return jnp.concatenate([ref[j + n, first : first + T, :] for n in range(u)], axis=0)


def quarter(c):
    return slice(c * 256, (c + 1) * 256)


def fold(x):
    return x.reshape(-1, 8, 256)


def probs_kernel(
    at_ref, r1_ref, q_ref, d_ref, other_ref, pay_ref, p_hbm, qs_ref, ds_ref,
    s_sc, dv_sc, qt_sc, sem
):
    at = at_ref[0]
    upper = (at >= 16).astype(jnp.int32)
    low = jnp.minimum(at, partner_of(at))
    high = jnp.maximum(at, partner_of(at))

    for h in range(GH):
        own = pl.ds(pl.multiple_of(upper * 1024 + h * T, T), T)
        qs_ref[upper, head(h), :] = q_ref[:, own]
        ds_ref[upper, head(h), :] = d_ref[:, own]
        qs_ref[1 - upper, head(h), :] = other_ref[0:T, head(h)]
        ds_ref[1 - upper, head(h), :] = other_ref[T : 2 * T, head(h)]
        qt_sc[upper, :, head(h)] = jnp.transpose(q_ref[:, own])
        qt_sc[1 - upper, :, head(h)] = jnp.transpose(other_ref[0:T, head(h)])

    dv_sc[...] = jnp.zeros_like(dv_sc)
    key = lax.broadcasted_iota(jnp.int32, (T, 256), 0)
    tok = lax.broadcasted_iota(jnp.int32, (T, 256), 1) & (T - 1)
    seen = key <= tok

    for sel in range(2):
        count = low if sel == 0 else high
        base = 0 if sel == 0 else low + 1

        def scores(j, u, top, diag=False, sel=sel, base=base):
            k = rows_of(r1_ref, j, u, SR + DR)
            tops = []
            for c in range(4):
                s = mm(k, qt_sc[sel, :, quarter(c)])
                if diag:
                    s = jnp.where(seen, s, NEG)
                s_sc[pl.ds(base + j, u), :, quarter(c)] = s.reshape(u, T, 256)
                tops.append(jnp.maximum(top[c], jnp.max(fold(s), axis=0)))
            return tuple(tops)

        top = tuple(jnp.full((8, 256), NEG, F32) for _ in range(4))
        top = steps_of(count, scores, top)
        top = scores(count, 1, top, True)
        peak = [jnp.max(t, axis=0, keepdims=True) for t in top]

        def weigh(j, u, tot, base=base, peak=peak):
            tots = []
            for c in range(4):
                p = jnp.exp((s_sc[pl.ds(base + j, u), :, quarter(c)] - peak[c]) * SCALE)
                tots.append(tot[c] + jnp.sum(fold(p), axis=0))
            return tuple(tots)

        tot = tuple(jnp.zeros((8, 256), F32) for _ in range(4))
        tot = steps_of(count + 1, weigh, tot)
        shift = [
            peak[c] * SCALE + jnp.log(jnp.sum(tot[c], axis=0, keepdims=True)) for c in range(4)
        ]

        def spread(j, u, none, sel=sel, base=base, shift=shift):
            ps = []
            at_b = pl.ds(base + j, u)
            for c in range(4):
                p = jnp.exp(s_sc[at_b, :, quarter(c)] * SCALE - shift[c])
                s_sc[at_b, :, quarter(c)] = p
                ps.append(p.astype(BF).reshape(u * T, 256))
            term = mm(jnp.concatenate(ps, axis=1), ds_ref[sel])
            dv_sc[pl.ds(j, u)] = dv_sc[pl.ds(j, u)] + term.reshape(u, T, T)
            pltpu.make_async_copy(s_sc.at[at_b], p_hbm.at[at_b], sem).start()
            return none

        steps_of(count + 1, spread, 0)

    run = jnp.zeros((SR, T), F32)
    for c in range(32):
        pay_ref[c, 0:SR, :] = run.astype(BF)
        run = decay_of(r1_ref, c) * run + r1_ref[c, 0:SR, :].astype(F32)
    for c in range(32):
        pay_ref[c, SR : SR + T, :] = dv_sc[c].astype(BF)

    def finish(b, none):
        pltpu.make_async_copy(s_sc.at[b], p_hbm.at[b], sem).wait()
        return none

    lax.fori_loop(0, low + high + 2, finish, 0)


def split(x):
    big = x.astype(BF)
    return big, (x - big.astype(F32)).astype(BF)


def values_kernel(
    x_ref, b_ref, c_ref, dt_ref, a_ref, skip_ref, r2_ref, w_ref, out_ref, y_sc
):
    cum = sums_by_token(dt_ref, a_ref)
    cum_t, dt_t = sums_by_head(cum), dt_ref[...]
    grow = jnp.exp(cum)
    lower = lower_tri()
    for g in range(2):
        cb = mm(c_ref[:, head(g)], b_ref[:, head(g)], NT)
        for h in range(g * GH, (g + 1) * GH):
            gap = cum[:, h : h + 1] - cum_t[h : h + 1, :]
            mix = cb * jnp.exp(jnp.where(lower, gap, NEG)) * dt_t[h : h + 1, :]
            x = x_ref[:, head(h)]
            enter = jnp.concatenate([r2_ref[2 * h, 0:SR, :], r2_ref[2 * h + 1, 0:SR, :]], 0)
            mix, rest = split(mix)
            y = mm(mix, x) + mm(rest, x) + skip_ref[:, h : h + 1] * x.astype(F32)
            y = y + grow[:, h : h + 1] * mm(c_ref[:, head(g)], enter, NT)
            y_sc[:, head(h)] = y.astype(BF)
    dv = []
    for k in range(2):
        acc = r2_ref[16 * k, SR : SR + T, :].astype(F32)
        for s in range(1, 16):
            acc = acc + r2_ref[16 * k + s, SR : SR + T, :].astype(F32)
        dv.append(acc.astype(BF))
    for d in range(4):
        out_ref[d, :, 0:256] = mm(y_sc[...], w_ref[:, quarter(d)]).astype(BF)
        out_ref[d, :, 256:384] = dv[0]
        out_ref[d, :, 384:512] = dv[1]


def back_kernel(r3_ref, w_ref, c_ref, dt_ref, a_ref, pay_ref, dy_ref):
    values = r3_ref[0, :, 0:256].astype(F32)
    for s in range(1, 4):
        values = values + r3_ref[s, :, 0:256].astype(F32)
    values = values.astype(BF)
    for d in range(32):
        pay_ref[d, SR : SR + T, :] = values[:, head(d // 16)]
    vg = jnp.concatenate([r3_ref[s, :, 256:512] for s in range(4)], axis=1)
    grow = jnp.exp(sums_by_token(dt_ref, a_ref))
    for pair in range(NH // 2):
        both = mm(vg, w_ref[quarter(pair), :], NT)
        dy_ref[:, quarter(pair)] = both
        for n in range(2):
            h = 2 * pair + n
            grown = (both[:, head(n)] * grow[:, h : h + 1]).astype(BF)
            eg = mm(grown, c_ref[:, head(h // GH)], TN).astype(BF)
            pay_ref[2 * h, 0:SR, :] = eg[0:SR]
            pay_ref[2 * h + 1, 0:SR, :] = eg[SR:T]


def grads_kernel(
    at_ref, r1_ref, r4_ref, qs_ref, ds_ref, p_hbm, pay_ref, o_ref, send_ref,
    p_sc, dp_sc, o_sc, dq_sc, dk_sc, dt_sc, sem
):
    at = at_ref[0]
    upper = (at >= 16).astype(jnp.int32)
    low = jnp.minimum(at, partner_of(at))
    high = jnp.maximum(at, partner_of(at))

    def begin(b, none):
        pltpu.make_async_copy(p_hbm.at[b], p_sc.at[b], sem.at[b]).start()
        return none

    lax.fori_loop(0, low + high + 2, begin, 0)

    run = jnp.zeros((SR, T), F32)
    for c in range(31, -1, -1):
        pay_ref[c, 0:SR, :] = run.astype(BF)
        run = decay_of(r1_ref, c) * run + r4_ref[c, 0:SR, :].astype(F32)

    for sel in range(2):
        for h in range(GH):
            dt_sc[sel, :, head(h)] = jnp.transpose(ds_ref[sel, head(h), :])
    dk_sc[...] = jnp.zeros_like(dk_sc)
    o_sc[...] = jnp.zeros_like(o_sc)
    dq_sc[...] = jnp.zeros_like(dq_sc)
    for sel in range(2):
        count = low if sel == 0 else high
        base = 0 if sel == 0 else low + 1

        def first(j, u, delta, sel=sel, base=base):
            for n in range(u):
                b = base + j + n
                pltpu.make_async_copy(p_hbm.at[b], p_sc.at[b], sem.at[b]).wait()
            at_b = pl.ds(base + j, u)
            v = rows_of(r4_ref, j, u, SR)
            v_t = jnp.transpose(v)
            deltas = []
            for c in range(4):
                p = p_sc[at_b, :, quarter(c)].astype(BF).reshape(u * T, 256)
                dp = mm(v, dt_sc[sel, :, quarter(c)])
                dp_sc[at_b, :, quarter(c)] = dp.reshape(u, T, 256)
                term = p.astype(F32) * dp
                deltas.append(delta[c] + jnp.sum(fold(term), axis=0))
                o_sc[sel, :, quarter(c)] += mm(v_t, p)
            return tuple(deltas)

        delta = tuple(jnp.zeros((8, 256), F32) for _ in range(4))
        delta = steps_of(count + 1, first, delta)
        delta = [jnp.sum(t, axis=0, keepdims=True) for t in delta]

        def second(j, u, none, sel=sel, base=base, delta=delta):
            at_b = pl.ds(base + j, u)
            k_t = jnp.transpose(rows_of(r1_ref, j, u, SR + DR))
            parts = []
            for c in range(4):
                ds = p_sc[at_b, :, quarter(c)] * (dp_sc[at_b, :, quarter(c)] - delta[c])
                ds = ds.astype(BF).reshape(u * T, 256)
                dq_sc[sel, :, quarter(c)] += mm(k_t, ds)
                parts.append(ds)
            term = mm(jnp.concatenate(parts, axis=1), qs_ref[sel])
            dk_sc[pl.ds(j, u)] = dk_sc[pl.ds(j, u)] + term.reshape(u, T, T)
            return none

        steps_of(count + 1, second, 0)

    for c in range(32):
        pay_ref[c, SR : SR + T, :] = dk_sc[c].astype(BF)
    for h in range(GH):
        o_ref[0:T, head(h)] = jnp.transpose(o_sc[upper, :, head(h)])
        o_ref[T : 2 * T, head(h)] = jnp.transpose(dq_sc[upper, :, head(h)]) * SCALE
        send_ref[0:T, head(h)] = jnp.transpose(o_sc[1 - upper, :, head(h)]).astype(BF)
        send_ref[T : 2 * T, head(h)] = (
            jnp.transpose(dq_sc[1 - upper, :, head(h)]) * SCALE
        ).astype(BF)


def local_kernel(
    x_ref, b_ref, c_ref, dt_ref, a_ref, skip_ref, dy_ref, r2_ref, gx_ref, gb_ref, gc_ref
):
    cum = sums_by_token(dt_ref, a_ref)
    cum_t, dt_t = sums_by_head(cum), dt_ref[...]
    grow = jnp.exp(cum)
    lower = lower_tri()
    for g in range(2):
        b = b_ref[:, head(g)]
        cc = c_ref[:, head(g)]
        cb = mm(cc, b, NT)
        mixed = jnp.zeros((T, T), F32)
        gc = jnp.zeros((T, T), F32)
        for h in range(g * GH, (g + 1) * GH):
            gap = cum[:, h : h + 1] - cum_t[h : h + 1, :]
            decay = jnp.exp(jnp.where(lower, gap, NEG)) * dt_t[h : h + 1, :]
            mix = (cb * decay).astype(BF)
            x = x_ref[:, head(h)]
            dy = dy_ref[:, head(h)]
            dyb = dy.astype(BF)
            enter = jnp.concatenate([r2_ref[2 * h, 0:SR, :], r2_ref[2 * h + 1, 0:SR, :]], 0)
            gx_ref[:, head(h)] = mm(mix, dyb, TN) + skip_ref[:, h : h + 1] * dy
            mixed = mixed + mm(dyb, x, NT) * decay
            gc = gc + grow[:, h : h + 1] * mm(dyb, enter)
        mixed = mixed.astype(BF)
        gb_ref[:, head(g)] = mm(mixed, cc, TN)
        gc_ref[:, head(g)] = gc + mm(mixed, b)


def final_kernel(
    x_ref, b_ref, dt_ref, a_ref, gx0_ref, gb0_ref, r5_ref, gx_ref, gb_ref, gk_ref
):
    cum = sums_by_token(dt_ref, a_ref)
    weight = jnp.exp(cum[T - 1 : T, :] - cum) * steps_by_token(dt_ref)
    for g in range(2):
        b = b_ref[:, head(g)]
        gb = gb0_ref[:, head(g)]
        for h in range(g * GH, (g + 1) * GH):
            sg = jnp.concatenate([r5_ref[2 * h, 0:SR, :], r5_ref[2 * h + 1, 0:SR, :]], 0)
            gx_ref[:, head(h)] = gx0_ref[:, head(h)] + weight[:, h : h + 1] * mm(b, sg, NT)
            gb = gb + weight[:, h : h + 1] * mm(x_ref[:, head(h)], sg)
        gb_ref[:, head(g)] = gb
    for k in range(2):
        acc = r5_ref[16 * k, SR : SR + T, :].astype(F32)
        for s in range(1, 16):
            acc = acc + r5_ref[16 * k + s, SR : SR + T, :].astype(F32)
        gk_ref[:, head(k)] = acc * SCALE


VM = pl.BlockSpec(memory_space=pltpu.VMEM)
SM = pl.BlockSpec(memory_space=pltpu.SMEM)
ANY = pl.BlockSpec(memory_space=pl.ANY)


def call(kernel, outs, scratch, name, mib, flops, nbytes, *args, far_in=(), far_out=()):
    places = [SM if a.dtype == jnp.int32 else VM for a in args]
    return pl.pallas_call(
        kernel,
        name=name,
        out_shape=[jax.ShapeDtypeStruct(s, d) for s, d in outs],
        in_specs=[ANY if n in far_in else place for n, place in enumerate(places)],
        out_specs=[ANY if n in far_out else VM for n in range(len(outs))],
        scratch_shapes=scratch,
        cost_estimate=pl.CostEstimate(
            flops=flops, bytes_accessed=nbytes, transcendentals=0
        ),
        compiler_params=pltpu.CompilerParams(vmem_limit_bytes=mib << 20),
    )(*args)


def over_ctx(pay):
    return lax.all_to_all(pay, "ctx", 0, 0, tiled=True)


def body(
    mamba_x, mamba_b, mamba_c, step_dt, decay_a, skip_d, value_weight, queries, keys, out_grad
):
    at = lax.axis_index("ctx")
    at1 = at.astype(jnp.int32).reshape(1)
    upper = at >= 16
    a_row = decay_a.reshape(1, NH)
    steps = step_dt.T
    skip_row = skip_d.reshape(1, NH)
    swap = [(i, partner_of(i)) for i in range(32)]

    away = jnp.concatenate(
        [
            jnp.where(upper, queries[:, :1024], queries[:, 1024:]),
            jnp.where(upper, out_grad[:, :1024], out_grad[:, 1024:]),
        ],
        axis=0,
    )
    other = lax.ppermute(away, "ctx", swap)
    (pay1,) = call(
        state_kernel, [((32, SR + DR + T, T), BF)], [], "block_states", 62, 1 << 34, 1 << 22,
        mamba_x, mamba_b, steps, a_row, keys,
    )
    r1 = over_ctx(pay1)
    pay2, probs, qs, ds = call(
        probs_kernel,
        [((32, SR + T, T), BF), ((NB, T, 1024), F32), ((2, 1024, T), BF), ((2, 1024, T), BF)],
        [
            pltpu.VMEM((NB, T, 1024), F32), pltpu.VMEM((32, T, T), F32),
            pltpu.VMEM((2, T, 1024), BF), pltpu.SemaphoreType.DMA,
        ],
        "probs", 48, 1 << 32, 1 << 25, at1, r1, queries, out_grad, other, far_out=(1,),
    )
    r2 = over_ctx(pay2)
    (pay3,) = call(
        values_kernel, [((4, T, 512), BF)], [pltpu.VMEM((T, 2048), BF)], "values", 24,
        1 << 30, 1 << 23,
        mamba_x, mamba_b, mamba_c, steps, a_row, skip_row, r2, value_weight,
    )
    r3 = lax.all_to_all(pay3, ("ch", "section"), 0, 0, tiled=True)
    pay4, dy = call(
        back_kernel, [((32, SR + T, T), BF), ((T, 2048), F32)], [], "value_back", 24, 1 << 30,
        1 << 23, r3, value_weight, mamba_c, steps, a_row,
    )
    r4 = over_ctx(pay4)
    gx0, gb0, grad_c = call(
        local_kernel,
        [((T, 2048), F32), ((T, 256), F32), ((T, 256), F32)], [], "mixer_local", 24,
        1 << 29, 1 << 23,
        mamba_x, mamba_b, mamba_c, steps, a_row, skip_row, dy, r2,
    )
    pay5, kept, send = call(
        grads_kernel,
        [((32, SR + T, T), BF), ((256, 1024), F32), ((256, 1024), BF)],
        [
            pltpu.VMEM((NB, T, 1024), F32), pltpu.VMEM((NB, T, 1024), F32),
            pltpu.VMEM((2, T, 1024), F32), pltpu.VMEM((2, T, 1024), F32),
            pltpu.VMEM((32, T, T), F32), pltpu.VMEM((2, T, 1024), BF),
            pltpu.SemaphoreType.DMA((NB,)),
        ],
        "attention_grads", 62, 1 << 32, 1 << 25, at1, r1, r4, qs, ds, probs, far_in=(5,),
    )
    back = lax.ppermute(send, "ctx", swap)
    r5 = over_ctx(pay5)
    grad_x, grad_b, grad_k = call(
        final_kernel,
        [((T, 2048), F32), ((T, 256), F32), ((T, 256), F32)],
        [], "mixer_grads", 24, 1 << 29, 1 << 23,
        mamba_x, mamba_b, steps, a_row, gx0, gb0, r5,
    )
    back = back.astype(F32)
    whole = jnp.where(
        upper, jnp.concatenate([back, kept], axis=1), jnp.concatenate([kept, back], axis=1)
    )
    return (whole[:T], whole[T:], grad_k, grad_x, grad_b, grad_c)


def solution(mesh):
    tokens = P("ctx", ("ch", "section"))
    heads = P(("ch", "section"))
    in_specs = (
        tokens, tokens, tokens, tokens, heads, heads, P(("ch", "section"), None),
        tokens, tokens, tokens,
    )
    return jax.shard_map(
        body, mesh=mesh, in_specs=in_specs, out_specs=(tokens,) * 6, check_vma=False
    )
```

```python
import math

import jax
import jax.numpy as jnp
from jax import lax
from jax.experimental import pallas as pl
from jax.experimental.pallas import tpu as pltpu
from jax.sharding import PartitionSpec as P

T = 128
NH = 16
GH = 8
F32 = jnp.float32
BF = jnp.bfloat16
HI = lax.Precision.HIGHEST
SCALE = 1.0 / math.sqrt(128.0)
SR = 64
DR = 16
NEG = -1e30
NB = 40

NN = (((1,), (0,)), ((), ()))
NT = (((1,), (1,)), ((), ()))
TN = (((0,), (0,)), ((), ()))


def mm(a, b, dims=NN):
    return lax.dot_general(a, b, dims, preferred_element_type=F32)


def mm_exact(a, b, dims=NN):
    return lax.dot_general(a, b, dims, precision=HI, preferred_element_type=F32)


def head(h):
    return slice(h * T, (h + 1) * T)


def lower_tri():
    row = lax.broadcasted_iota(jnp.int32, (T, T), 0)
    col = lax.broadcasted_iota(jnp.int32, (T, T), 1)
    return row >= col


def same_token():
    row = lax.broadcasted_iota(jnp.int32, (T, T), 0)
    col = lax.broadcasted_iota(jnp.int32, (T, T), 1)
    return (row == col).astype(F32)


def sums_by_token(dt_ref, a_ref):
    return -mm_exact(lower_tri().astype(F32), dt_ref[...], NT) * a_ref[...]


def sums_and_steps(dt_ref, a_ref):
    picks = jnp.concatenate([lower_tri().astype(F32), same_token()], axis=0)
    both = mm_exact(picks, dt_ref[...], NT)
    return -both[:T] * a_ref[...], both[T:]


def sums_by_head(cum):
    return mm_exact(cum, same_token(), TN)


def state_kernel(x_ref, b_ref, dt_ref, a_ref, k_ref, out_ref):
    cum, steps = sums_and_steps(dt_ref, a_ref)
    total = cum[T - 1 : T, :]
    weight = jnp.exp(total - cum) * steps
    first = total.astype(BF).astype(F32)
    second = (total - first).astype(BF).astype(F32)
    third = total - first - second
    row = lax.broadcasted_iota(jnp.int32, (DR, T), 0)
    for h in range(NH):
        g = h // GH
        xw = (x_ref[:, head(h)].astype(F32) * weight[:, h : h + 1]).astype(BF)
        state = mm(xw, b_ref[:, head(g)], TN).astype(BF)
        parts = jnp.where(
            row == 0,
            first[:, h : h + 1],
            jnp.where(row == 1, second[:, h : h + 1], third[:, h : h + 1]),
        ).astype(BF)
        for half in range(2):
            d = 2 * h + half
            out_ref[d, 0:SR, :] = state[half * SR : (half + 1) * SR]
            out_ref[d, SR : SR + DR, :] = parts
    for d in range(32):
        out_ref[d, SR + DR : SR + DR + T, :] = k_ref[:, head(d // 16)]


def partner_of(at):
    return at + 24 - 16 * (at // 8)


def decay_of(r1_ref, c):
    parts = r1_ref[c, SR : SR + DR, :].astype(F32)
    return jnp.exp(parts[0:1] + parts[1:2] + parts[2:3])


def steps_of(n, step, init):
    at = 0
    for size in (8, 4, 2, 1):
        whole = (n - at) // size
        init = lax.fori_loop(
            0, whole, lambda i, c, at=at, size=size: step(at + i * size, size, c), init
        )
        at = at + whole * size
    return init


def rows_of(ref, j, u, first):
    return jnp.concatenate([ref[j + n, first : first + T, :] for n in range(u)], axis=0)


def quarter(c):
    return slice(c * 256, (c + 1) * 256)


def fold(x):
    return x.reshape(-1, 8, 256)


def probs_kernel(
    at_ref, r1_ref, q_ref, d_ref, other_ref, pay_ref, p_hbm, qs_ref, ds_ref,
    s_sc, dv_sc, qt_sc, sem
):
    at = at_ref[0]
    upper = (at >= 16).astype(jnp.int32)
    low = jnp.minimum(at, partner_of(at))
    high = jnp.maximum(at, partner_of(at))

    for h in range(GH):
        own = pl.ds(pl.multiple_of(upper * 1024 + h * T, T), T)
        qs_ref[upper, head(h), :] = q_ref[:, own]
        ds_ref[upper, head(h), :] = d_ref[:, own]
        qs_ref[1 - upper, head(h), :] = other_ref[0:T, head(h)]
        ds_ref[1 - upper, head(h), :] = other_ref[T : 2 * T, head(h)]
        qt_sc[upper, :, head(h)] = jnp.transpose(q_ref[:, own])
        qt_sc[1 - upper, :, head(h)] = jnp.transpose(other_ref[0:T, head(h)])

    dv_sc[...] = jnp.zeros_like(dv_sc)
    key = lax.broadcasted_iota(jnp.int32, (T, 256), 0)
    tok = lax.broadcasted_iota(jnp.int32, (T, 256), 1) & (T - 1)
    seen = key <= tok

    for sel in range(2):
        count = low if sel == 0 else high
        base = 0 if sel == 0 else low + 1

        def scores(j, u, top, diag=False, sel=sel, base=base):
            k = rows_of(r1_ref, j, u, SR + DR)
            tops = []
            for c in range(4):
                s = mm(k, qt_sc[sel, :, quarter(c)])
                if diag:
                    s = jnp.where(seen, s, NEG)
                s_sc[pl.ds(base + j, u), :, quarter(c)] = s.reshape(u, T, 256)
                tops.append(jnp.maximum(top[c], jnp.max(fold(s), axis=0)))
            return tuple(tops)

        top = tuple(jnp.full((8, 256), NEG, F32) for _ in range(4))
        top = steps_of(count, scores, top)
        top = scores(count, 1, top, True)
        peak = [jnp.max(t, axis=0, keepdims=True) for t in top]

        def weigh(j, u, tot, base=base, peak=peak):
            tots = []
            for c in range(4):
                p = jnp.exp((s_sc[pl.ds(base + j, u), :, quarter(c)] - peak[c]) * SCALE)
                tots.append(tot[c] + jnp.sum(fold(p), axis=0))
            return tuple(tots)

        tot = tuple(jnp.zeros((8, 256), F32) for _ in range(4))
        tot = steps_of(count + 1, weigh, tot)
        shift = [
            peak[c] * SCALE + jnp.log(jnp.sum(tot[c], axis=0, keepdims=True)) for c in range(4)
        ]

        def spread(j, u, none, sel=sel, base=base, shift=shift):
            ps = []
            at_b = pl.ds(base + j, u)
            for c in range(4):
                p = jnp.exp(s_sc[at_b, :, quarter(c)] * SCALE - shift[c])
                s_sc[at_b, :, quarter(c)] = p
                ps.append(p.astype(BF).reshape(u * T, 256))
            term = mm(jnp.concatenate(ps, axis=1), ds_ref[sel])
            dv_sc[pl.ds(j, u)] = dv_sc[pl.ds(j, u)] + term.reshape(u, T, T)
            pltpu.make_async_copy(s_sc.at[at_b], p_hbm.at[at_b], sem).start()
            return none

        steps_of(count + 1, spread, 0)

    run = jnp.zeros((SR, T), F32)
    for c in range(32):
        pay_ref[c, 0:SR, :] = run.astype(BF)
        run = decay_of(r1_ref, c) * run + r1_ref[c, 0:SR, :].astype(F32)
    for c in range(32):
        pay_ref[c, SR : SR + T, :] = dv_sc[c].astype(BF)

    def finish(b, none):
        pltpu.make_async_copy(s_sc.at[b], p_hbm.at[b], sem).wait()
        return none

    lax.fori_loop(0, low + high + 2, finish, 0)


def split(x):
    big = x.astype(BF)
    return big, (x - big.astype(F32)).astype(BF)


def values_kernel(
    x_ref, b_ref, c_ref, dt_ref, a_ref, skip_ref, r2_ref, w_ref, out_ref, y_sc
):
    cum = sums_by_token(dt_ref, a_ref)
    cum_t, dt_t = sums_by_head(cum), dt_ref[...]
    grow = jnp.exp(cum)
    lower = lower_tri()
    for g in range(2):
        cb = mm(c_ref[:, head(g)], b_ref[:, head(g)], NT)
        for h in range(g * GH, (g + 1) * GH):
            gap = cum[:, h : h + 1] - cum_t[h : h + 1, :]
            mix = cb * jnp.exp(jnp.where(lower, gap, NEG)) * dt_t[h : h + 1, :]
            x = x_ref[:, head(h)]
            enter = jnp.concatenate([r2_ref[2 * h, 0:SR, :], r2_ref[2 * h + 1, 0:SR, :]], 0)
            mix, rest = split(mix)
            y = mm(mix, x) + mm(rest, x) + skip_ref[:, h : h + 1] * x.astype(F32)
            y = y + grow[:, h : h + 1] * mm(c_ref[:, head(g)], enter, NT)
            y_sc[:, head(h)] = y.astype(BF)
    dv = []
    for k in range(2):
        acc = r2_ref[16 * k, SR : SR + T, :].astype(F32)
        for s in range(1, 16):
            acc = acc + r2_ref[16 * k + s, SR : SR + T, :].astype(F32)
        dv.append(acc.astype(BF))
    for d in range(4):
        out_ref[d, :, 0:256] = mm(y_sc[...], w_ref[:, quarter(d)]).astype(BF)
        out_ref[d, :, 256:384] = dv[0]
        out_ref[d, :, 384:512] = dv[1]


def back_kernel(r3_ref, w_ref, c_ref, dt_ref, a_ref, pay_ref, dy_ref):
    values = r3_ref[0, :, 0:256].astype(F32)
    for s in range(1, 4):
        values = values + r3_ref[s, :, 0:256].astype(F32)
    values = values.astype(BF)
    for d in range(32):
        pay_ref[d, SR : SR + T, :] = values[:, head(d // 16)]
    vg = jnp.concatenate([r3_ref[s, :, 256:512] for s in range(4)], axis=1)
    grow = jnp.exp(sums_by_token(dt_ref, a_ref))
    for pair in range(NH // 2):
        both = mm(vg, w_ref[quarter(pair), :], NT)
        dy_ref[:, quarter(pair)] = both
        for n in range(2):
            h = 2 * pair + n
            grown = (both[:, head(n)] * grow[:, h : h + 1]).astype(BF)
            eg = mm(grown, c_ref[:, head(h // GH)], TN).astype(BF)
            pay_ref[2 * h, 0:SR, :] = eg[0:SR]
            pay_ref[2 * h + 1, 0:SR, :] = eg[SR:T]


def grads_kernel(
    at_ref, r1_ref, r4_ref, qs_ref, ds_ref, p_hbm, pay_ref, o_ref, send_ref,
    p_sc, dp_sc, o_sc, dq_sc, dk_sc, dt_sc, sem
):
    at = at_ref[0]
    upper = (at >= 16).astype(jnp.int32)
    low = jnp.minimum(at, partner_of(at))
    high = jnp.maximum(at, partner_of(at))

    def begin(b, none):
        pltpu.make_async_copy(p_hbm.at[b], p_sc.at[b], sem.at[b]).start()
        return none

    lax.fori_loop(0, low + high + 2, begin, 0)

    run = jnp.zeros((SR, T), F32)
    for c in range(31, -1, -1):
        pay_ref[c, 0:SR, :] = run.astype(BF)
        run = decay_of(r1_ref, c) * run + r4_ref[c, 0:SR, :].astype(F32)

    for sel in range(2):
        for h in range(GH):
            dt_sc[sel, :, head(h)] = jnp.transpose(ds_ref[sel, head(h), :])
    dk_sc[...] = jnp.zeros_like(dk_sc)
    o_sc[...] = jnp.zeros_like(o_sc)
    dq_sc[...] = jnp.zeros_like(dq_sc)
    for sel in range(2):
        count = low if sel == 0 else high
        base = 0 if sel == 0 else low + 1

        def first(j, u, delta, sel=sel, base=base):
            for n in range(u):
                b = base + j + n
                pltpu.make_async_copy(p_hbm.at[b], p_sc.at[b], sem.at[b]).wait()
            at_b = pl.ds(base + j, u)
            v = rows_of(r4_ref, j, u, SR)
            v_t = jnp.transpose(v)
            deltas = []
            for c in range(4):
                p = p_sc[at_b, :, quarter(c)].astype(BF).reshape(u * T, 256)
                dp = mm(v, dt_sc[sel, :, quarter(c)])
                dp_sc[at_b, :, quarter(c)] = dp.reshape(u, T, 256)
                term = p.astype(F32) * dp
                deltas.append(delta[c] + jnp.sum(fold(term), axis=0))
                o_sc[sel, :, quarter(c)] += mm(v_t, p)
            return tuple(deltas)

        delta = tuple(jnp.zeros((8, 256), F32) for _ in range(4))
        delta = steps_of(count + 1, first, delta)
        delta = [jnp.sum(t, axis=0, keepdims=True) for t in delta]

        def second(j, u, none, sel=sel, base=base, delta=delta):
            at_b = pl.ds(base + j, u)
            k_t = jnp.transpose(rows_of(r1_ref, j, u, SR + DR))
            parts = []
            for c in range(4):
                ds = p_sc[at_b, :, quarter(c)] * (dp_sc[at_b, :, quarter(c)] - delta[c])
                ds = ds.astype(BF).reshape(u * T, 256)
                dq_sc[sel, :, quarter(c)] += mm(k_t, ds)
                parts.append(ds)
            term = mm(jnp.concatenate(parts, axis=1), qs_ref[sel])
            dk_sc[pl.ds(j, u)] = dk_sc[pl.ds(j, u)] + term.reshape(u, T, T)
            return none

        steps_of(count + 1, second, 0)

    for c in range(32):
        pay_ref[c, SR : SR + T, :] = dk_sc[c].astype(BF)
    for h in range(GH):
        o_ref[0:T, head(h)] = jnp.transpose(o_sc[upper, :, head(h)])
        o_ref[T : 2 * T, head(h)] = jnp.transpose(dq_sc[upper, :, head(h)]) * SCALE
        send_ref[0:T, head(h)] = jnp.transpose(o_sc[1 - upper, :, head(h)]).astype(BF)
        send_ref[T : 2 * T, head(h)] = (
            jnp.transpose(dq_sc[1 - upper, :, head(h)]) * SCALE
        ).astype(BF)


def local_kernel(
    x_ref, b_ref, c_ref, dt_ref, a_ref, skip_ref, dy_ref, r2_ref, gx_ref, gb_ref, gc_ref,
    weight_ref
):
    cum, steps = sums_and_steps(dt_ref, a_ref)
    weight_ref[...] = jnp.exp(cum[T - 1 : T, :] - cum) * steps
    cum_t, dt_t = sums_by_head(cum), dt_ref[...]
    grow = jnp.exp(cum)
    lower = lower_tri()
    for g in range(2):
        b = b_ref[:, head(g)]
        cc = c_ref[:, head(g)]
        cb = mm(cc, b, NT)
        mixed = jnp.zeros((T, T), F32)
        gc = jnp.zeros((T, T), F32)
        for h in range(g * GH, (g + 1) * GH):
            gap = cum[:, h : h + 1] - cum_t[h : h + 1, :]
            decay = jnp.exp(jnp.where(lower, gap, NEG)) * dt_t[h : h + 1, :]
            mix = (cb * decay).astype(BF)
            x = x_ref[:, head(h)]
            dy = dy_ref[:, head(h)]
            dyb = dy.astype(BF)
            enter = jnp.concatenate([r2_ref[2 * h, 0:SR, :], r2_ref[2 * h + 1, 0:SR, :]], 0)
            gx_ref[:, head(h)] = mm(mix, dyb, TN) + skip_ref[:, h : h + 1] * dy
            mixed = mixed + mm(dyb, x, NT) * decay
            gc = gc + grow[:, h : h + 1] * mm(dyb, enter)
        mixed = mixed.astype(BF)
        gb_ref[:, head(g)] = mm(mixed, cc, TN)
        gc_ref[:, head(g)] = gc + mm(mixed, b)


def final_kernel(
    x_ref, b_ref, weight_ref, gx0_ref, gb0_ref, r5_ref, gx_ref, gb_ref, gk_ref
):
    weight = weight_ref[...]
    for g in range(2):
        b = b_ref[:, head(g)]
        gb = gb0_ref[:, head(g)]
        for h in range(g * GH, (g + 1) * GH):
            sg = jnp.concatenate([r5_ref[2 * h, 0:SR, :], r5_ref[2 * h + 1, 0:SR, :]], 0)
            gx_ref[:, head(h)] = gx0_ref[:, head(h)] + weight[:, h : h + 1] * mm(b, sg, NT)
            gb = gb + weight[:, h : h + 1] * mm(x_ref[:, head(h)], sg)
        gb_ref[:, head(g)] = gb
    for k in range(2):
        acc = r5_ref[16 * k, SR : SR + T, :].astype(F32)
        for s in range(1, 16):
            acc = acc + r5_ref[16 * k + s, SR : SR + T, :].astype(F32)
        gk_ref[:, head(k)] = acc * SCALE


VM = pl.BlockSpec(memory_space=pltpu.VMEM)
SM = pl.BlockSpec(memory_space=pltpu.SMEM)
ANY = pl.BlockSpec(memory_space=pl.ANY)


def call(kernel, outs, scratch, name, mib, flops, nbytes, *args, far_in=(), far_out=()):
    places = [SM if a.dtype == jnp.int32 else VM for a in args]
    return pl.pallas_call(
        kernel,
        name=name,
        out_shape=[jax.ShapeDtypeStruct(s, d) for s, d in outs],
        in_specs=[ANY if n in far_in else place for n, place in enumerate(places)],
        out_specs=[ANY if n in far_out else VM for n in range(len(outs))],
        scratch_shapes=scratch,
        cost_estimate=pl.CostEstimate(
            flops=flops, bytes_accessed=nbytes, transcendentals=0
        ),
        compiler_params=pltpu.CompilerParams(vmem_limit_bytes=mib << 20),
    )(*args)


def over_ctx(pay):
    return lax.all_to_all(pay, "ctx", 0, 0, tiled=True)


def body(
    mamba_x, mamba_b, mamba_c, step_dt, decay_a, skip_d, value_weight, queries, keys, out_grad
):
    at = lax.axis_index("ctx")
    at1 = at.astype(jnp.int32).reshape(1)
    upper = at >= 16
    a_row = decay_a.reshape(1, NH)
    steps = step_dt.T
    skip_row = skip_d.reshape(1, NH)
    swap = [(i, partner_of(i)) for i in range(32)]

    away = jnp.concatenate(
        [
            jnp.where(upper, queries[:, :1024], queries[:, 1024:]),
            jnp.where(upper, out_grad[:, :1024], out_grad[:, 1024:]),
        ],
        axis=0,
    )
    other = lax.ppermute(away, "ctx", swap)
    (pay1,) = call(
        state_kernel, [((32, SR + DR + T, T), BF)], [], "block_states", 62, 1 << 34, 1 << 22,
        mamba_x, mamba_b, steps, a_row, keys,
    )
    r1 = over_ctx(pay1)
    pay2, probs, qs, ds = call(
        probs_kernel,
        [((32, SR + T, T), BF), ((NB, T, 1024), F32), ((2, 1024, T), BF), ((2, 1024, T), BF)],
        [
            pltpu.VMEM((NB, T, 1024), F32), pltpu.VMEM((32, T, T), F32),
            pltpu.VMEM((2, T, 1024), BF), pltpu.SemaphoreType.DMA,
        ],
        "probs", 48, 1 << 32, 1 << 25, at1, r1, queries, out_grad, other, far_out=(1,),
    )
    r2 = over_ctx(pay2)
    (pay3,) = call(
        values_kernel, [((4, T, 512), BF)], [pltpu.VMEM((T, 2048), BF)], "values", 24,
        1 << 30, 1 << 23,
        mamba_x, mamba_b, mamba_c, steps, a_row, skip_row, r2, value_weight,
    )
    r3 = lax.all_to_all(pay3, ("ch", "section"), 0, 0, tiled=True)
    pay4, dy = call(
        back_kernel, [((32, SR + T, T), BF), ((T, 2048), F32)], [], "value_back", 24, 1 << 30,
        1 << 23, r3, value_weight, mamba_c, steps, a_row,
    )
    r4 = over_ctx(pay4)
    gx0, gb0, grad_c, weight = call(
        local_kernel,
        [((T, 2048), F32), ((T, 256), F32), ((T, 256), F32), ((T, NH), F32)], [], "mixer_local", 24,
        1 << 29, 1 << 23,
        mamba_x, mamba_b, mamba_c, steps, a_row, skip_row, dy, r2,
    )
    pay5, kept, send = call(
        grads_kernel,
        [((32, SR + T, T), BF), ((256, 1024), F32), ((256, 1024), BF)],
        [
            pltpu.VMEM((NB, T, 1024), F32), pltpu.VMEM((NB, T, 1024), F32),
            pltpu.VMEM((2, T, 1024), F32), pltpu.VMEM((2, T, 1024), F32),
            pltpu.VMEM((32, T, T), F32), pltpu.VMEM((2, T, 1024), BF),
            pltpu.SemaphoreType.DMA((NB,)),
        ],
        "attention_grads", 62, 1 << 32, 1 << 25, at1, r1, r4, qs, ds, probs, far_in=(5,),
    )
    back = lax.ppermute(send, "ctx", swap)
    r5 = over_ctx(pay5)
    grad_x, grad_b, grad_k = call(
        final_kernel,
        [((T, 2048), F32), ((T, 256), F32), ((T, 256), F32)],
        [], "mixer_grads", 24, 1 << 29, 1 << 23,
        mamba_x, mamba_b, weight, gx0, gb0, r5,
    )
    kept, grad_k = lax.optimization_barrier((kept, grad_k))

    def joined(first):
        mine = kept[first : first + T]
        theirs = back[first : first + T].astype(F32)
        return jnp.where(
            upper,
            jnp.concatenate([theirs, mine], axis=1),
            jnp.concatenate([mine, theirs], axis=1),
        )

    return (joined(0), joined(T), grad_k, grad_x, grad_b, grad_c)


def solution(mesh):
    tokens = P("ctx", ("ch", "section"))
    heads = P(("ch", "section"))
    in_specs = (
        tokens, tokens, tokens, tokens, heads, heads, P(("ch", "section"), None),
        tokens, tokens, tokens,
    )
    return jax.shard_map(
        body, mesh=mesh, in_specs=in_specs, out_specs=(tokens,) * 6, check_vma=False
    )
```
